32 devices in a mesh: sec: 2 (over core), grp: 4 (over y, x), cp: 4 (over z).
Axes of the slice: x: 2, y: 2, z: 4, core: 2. Of those that a mesh axis runs over, the one named last changes fastest.
Arguments:
- prompt_states: bfloat16 [8, 768, 8192], P('grp', 'cp'), may hold values from -6 to 6
- prompt_queries: bfloat16 [8, 768, 1024], P('grp', 'cp', 'sec'), may hold values from -180 to 180
- decode_states: bfloat16 [3, 128, 8192], P(None, 'grp'), may hold values from -6 to 6
- decode_queries: bfloat16 [3, 128, 1024], P(None, 'grp', 'sec'), may hold values from -180 to 180
- latent_down: bfloat16 [8192, 256], P(None, 'sec'), may hold values from -0.0625 to 0.0625
- key_up: bfloat16 [128, 1024], P(None, 'sec'), may hold values from -0.5 to 0.5
- value_up: bfloat16 [128, 1024], P(None, 'sec'), may hold values from -0.5 to 0.5
- prompt_lengths: int32 [8], P('grp'), may hold values from 192 to 768
- block_order: int32 [8], replicated, may hold values from 0 to 7, each once
- page_owner: int32 [4, 4, 24], P('grp'), may hold values from 0 to 3, as said below
- decode_context: int32 [128], P('grp'), may hold values from 96 to 768
Outputs:
- prefill_out: bfloat16 [8, 768, 1024], P('grp', 'cp', 'sec')
- decode_out: bfloat16 [3, 128, 1024], P(None, 'grp', 'sec')
- page_cache: bfloat16 [4, 4, 384, 256], P('grp', 'cp')
The draws below stay inside these ranges and needn't reach their ends.
Inputs may be any that keep to these rules, and one draw needn't show every extreme that they name: block_order names each block of a prompt once. page_owner[g, s, k] is an index along cp; every owner receives exactly 24 pages of its group, and at most 6 from one device.
All inputs are finite; a program needn't handle non-finite values.
Results may differ from the reference program's by a relative error of at most 0.012.
The reference program's roundings to bfloat16 on the way count: a program that leaves them out, or rounds other values in their place, can miss the bound.
Values may be sent and summed in bfloat16 or wider, within the bound.
A program may use at most 128 MiB of HBM per device.

```python
import jax
import jax.numpy as jnp
from jax import lax

D = 8192
HEADS = 8
HEAD = 128
RANK = 128
BLOCK = 96
PAGE = 16
PPG = 2
ROW_GRP = 32
STEPS = 3
SEQ = 768
PROMPTS = 8
ROWS = 128
PAGES_DEV = 24
GROUPS = 4
OWNERS = 4
BLOCKS = 8


def spread_queries(draw_key, out_shape):
    base_key = jax.random.fold_in(draw_key, 0)
    return jnp.clip(2.5 * jax.random.normal(base_key, out_shape, jnp.float32), -20.0, 20.0).astype(jnp.bfloat16)


def draw_prompt_queries(key, part):
    return spread_queries(jax.random.fold_in(key, 11), (PROMPTS, SEQ, HEADS * HEAD))


def draw_decode_queries(key, part):
    return spread_queries(jax.random.fold_in(key, 23), (STEPS, ROWS, HEADS * HEAD))


def draw_page_owner(key, part):
    group_key, page_key = jax.random.split(jax.random.fold_in(key, 37))
    owner_perm = jax.vmap(lambda one_key: jax.random.permutation(one_key, OWNERS))(jax.random.split(group_key, GROUPS))
    page_perm = jax.vmap(lambda one_key: jax.random.permutation(one_key, PAGES_DEV))(jax.random.split(page_key, GROUPS * OWNERS))
    page_perm = page_perm.reshape(GROUPS, OWNERS, PAGES_DEV).astype(jnp.int32)
    shifted = (jnp.arange(OWNERS, dtype=jnp.int32)[None, :, None] + page_perm) % OWNERS
    spread = jnp.broadcast_to(owner_perm.astype(jnp.int32)[:, None, :], (GROUPS, OWNERS, OWNERS))
    return jnp.take_along_axis(spread, shifted, axis=2).astype(jnp.int32)


def with_ends(result, key, least, largest):
    longest = result.shape.index(max(result.shape))
    spots = []
    for shift in (0, 1):
        where = [jax.random.randint(jax.random.fold_in(key, axis), (), 0, length) for axis, length in enumerate(result.shape)]
        where[longest] = (where[longest] + shift) % result.shape[longest]
        spots.append(tuple(where))
    return result.at[spots[0]].set(least).at[spots[1]].set(largest)


def steps_of(rng, shape, shards, least, top_value):
    def one(axis_at, shards_of):
        draws = jax.random.uniform(jax.random.fold_in(jax.random.fold_in(rng, 6), axis_at), (shards_of,), jnp.float32, least / len(shards), top_value / len(shards))
        return jnp.repeat(jnp.exp(draws), shape[axis_at] // shards_of).reshape((-1,) + (1,) * (len(shape) - axis_at - 1))

    gain = one(*shards[0])
    for cut in shards[1:]:
        gain = gain * one(*cut)
    return gain


def normal_values(rng, dims, scale, limit, pieces=(), kind=jnp.bfloat16):
    array = scale * jax.random.normal(rng, dims, jnp.float32)
    if pieces:
        array = array * steps_of(rng, dims, pieces, -0.22, 0.18)
    return jnp.clip(array, -limit, limit).astype(kind)


def setup_inputs(seed: int = 0) -> dict:
    splits = jax.random.split(jax.random.key(seed), 12)
    prompt_states = normal_values(splits[0], (PROMPTS, SEQ, D), 1.0, 6.0, ((0, 4), (1, 4)))
    prompt_queries = draw_prompt_queries(jax.random.fold_in(splits[11], 71), 0)
    decode_states = normal_values(splits[2], (STEPS, ROWS, D), 1.0, 6.0, ((1, 4),))
    decode_queries = draw_decode_queries(jax.random.fold_in(splits[11], 71), 0)
    latent_down = normal_values(splits[4], (D, 2 * RANK), D ** -0.5, 0.0625, ((1, 2),))
    key_up = normal_values(splits[5], (RANK, HEADS * HEAD), RANK ** -0.5, 0.5, ((1, 2),))
    value_up = normal_values(splits[6], (RANK, HEADS * HEAD), RANK ** -0.5, 0.5, ((1, 2),))
    prompt_lengths = with_ends(jax.random.randint(splits[7], (PROMPTS,), SEQ // 4, SEQ + 1), jax.random.fold_in(splits[7], 1), SEQ // 4, SEQ).astype(jnp.int32)
    block_order = jax.random.permutation(splits[8], BLOCKS).astype(jnp.int32)
    page_owner = draw_page_owner(jax.random.fold_in(splits[11], 71), 0)
    decode_context = with_ends(jax.random.randint(splits[10], (ROWS,), SEQ // 8, SEQ + 1), jax.random.fold_in(splits[10], 1), SEQ // 8, SEQ).astype(jnp.int32)
    return {"prompt_states": prompt_states, "prompt_queries": prompt_queries, "decode_states": decode_states, "decode_queries": decode_queries, "latent_down": latent_down, "key_up": key_up, "value_up": value_up, "prompt_lengths": prompt_lengths, "block_order": block_order, "page_owner": page_owner, "decode_context": decode_context}


NEG = -1e30


def stored_positions(block_order, stored_rows):
    return block_order[stored_rows // BLOCK] * BLOCK + stored_rows % BLOCK


def absorb(queries, key_up):
    row_count = queries.shape[0]
    q_parts = queries.astype(jnp.float32).reshape(row_count, HEADS, HEAD)
    u_parts = key_up.astype(jnp.float32).reshape(RANK, HEADS, HEAD)
    return jnp.einsum("nhd,rhd->hnr", q_parts, u_parts).astype(jnp.bfloat16)


def rebuild(latent_out, value_up):
    u_parts = value_up.astype(jnp.float32).reshape(RANK, HEADS, HEAD)
    rebuilt = jnp.einsum("hnr,rhd->nhd", latent_out.astype(jnp.float32), u_parts)
    return rebuilt.astype(jnp.bfloat16).reshape(latent_out.shape[1], HEADS * HEAD)


def attend(query_abs, key_rows, value_rows, key_mask):
    scores = jnp.dot(query_abs, key_rows.T, preferred_element_type=jnp.float32) * HEAD ** -0.5
    scores = jnp.where(key_mask, scores, NEG)
    row_peak = jnp.max(scores, axis=-1, keepdims=True)
    weights = jnp.where(key_mask, jnp.exp(scores - row_peak), 0.0)
    row_total = jnp.sum(weights, axis=-1, keepdims=True)
    weighted = jnp.dot(weights.astype(jnp.bfloat16), value_rows, preferred_element_type=jnp.float32)
    return (weighted / row_total).astype(jnp.bfloat16)


def reference(prompt_states, prompt_queries, decode_states, decode_queries, latent_down, key_up, value_up, prompt_lengths, block_order, page_owner, decode_context):
    latent = jnp.dot(prompt_states.reshape(PROMPTS * SEQ, D), latent_down, preferred_element_type=jnp.float32).astype(jnp.bfloat16).reshape(PROMPTS, SEQ, 2 * RANK)
    new_latent = jnp.dot(decode_states.reshape(STEPS * ROWS, D), latent_down, preferred_element_type=jnp.float32).astype(jnp.bfloat16).reshape(STEPS, ROWS, 2 * RANK)
    positions = stored_positions(block_order, jnp.arange(SEQ, dtype=jnp.int32))
    causal = positions[None, :] <= positions[:, None]

    def prefill_prompt(prompt_id):
        prompt_latent = latent[prompt_id]
        query_abs = absorb(prompt_queries[prompt_id], key_up)

        def one_head(head_abs):
            return attend(head_abs, prompt_latent[:, :RANK], prompt_latent[:, RANK:], causal)

        latent_out = lax.map(one_head, query_abs)
        rebuilt = rebuild(latent_out, value_up)
        live_rows = positions < prompt_lengths[prompt_id]
        return jnp.where(live_rows[:, None], rebuilt, jnp.zeros_like(rebuilt))

    prefill_out = lax.map(prefill_prompt, jnp.arange(PROMPTS, dtype=jnp.int32))

    step_ids = jnp.arange(STEPS, dtype=jnp.int32)
    own_mask = step_ids[None, :] <= step_ids[:, None]

    def decode_row(row_id):
        group_id = row_id // ROW_GRP
        prompt_id = group_id * PPG + (row_id % ROW_GRP) // (ROW_GRP // PPG)
        row_limit = jnp.minimum(decode_context[row_id], prompt_lengths[prompt_id])
        key_rows = jnp.concatenate([latent[prompt_id], new_latent[:, row_id]], axis=0)
        cache_mask = jnp.broadcast_to((positions < row_limit)[None, :], (STEPS, SEQ))
        key_mask = jnp.concatenate([cache_mask, own_mask], axis=1)
        query_abs = absorb(decode_queries[:, row_id], key_up)
        latent_out = jax.vmap(lambda head_abs: attend(head_abs, key_rows[:, :RANK], key_rows[:, RANK:], key_mask))(query_abs)
        return rebuild(latent_out, value_up)

    decode_out = jnp.transpose(lax.map(decode_row, jnp.arange(ROWS, dtype=jnp.int32)), (1, 0, 2))

    flat_owner = page_owner.reshape(GROUPS, OWNERS * PAGES_DEV)
    ranked = jnp.argsort(flat_owner, axis=1, stable=True).astype(jnp.int32)
    source = ranked // PAGES_DEV
    local_page = ranked % PAGES_DEV
    per_prompt = 2 * BLOCK // PAGE
    prompt_index = jnp.arange(GROUPS, dtype=jnp.int32)[:, None] * PPG + local_page // per_prompt
    first_row = source * (2 * BLOCK) + (local_page % per_prompt) * PAGE
    rows_index = first_row[..., None] + jnp.arange(PAGE, dtype=jnp.int32)
    page_cache = latent[prompt_index[..., None], rows_index].reshape(GROUPS, OWNERS, PAGES_DEV * PAGE, 2 * RANK)
    return prefill_out, decode_out, page_cache
```

```python
import functools
import math

import jax
import jax.numpy as jnp
from jax import lax
from jax.experimental import pallas as pl
from jax.experimental.pallas import tpu as pltpu
from jax.sharding import PartitionSpec as P

HEAD = 128
RANK = 128
BLOCK = 96
PAGE = 16
PPG = 2
ROW_GRP = 32
STEPS = 3
PAGES_DEV = 24


NEG = -1e30


def lookup(table_rows, indices):
    matches = indices[..., None] == jnp.arange(table_rows.shape[0], dtype=jnp.int32)
    return jnp.sum(jnp.where(matches, table_rows, 0), axis=-1)


def row_positions(block_order, stored_rows):
    return lookup(block_order, stored_rows // BLOCK) * BLOCK + stored_rows % BLOCK


def absorb(queries, key_up):
    row_count = queries.shape[0]
    head_count = key_up.shape[1] // HEAD
    q_parts = queries.reshape(row_count, head_count, HEAD)
    u_parts = key_up.reshape(RANK, head_count, HEAD)
    return jnp.einsum("nhd,rhd->hnr", q_parts, u_parts, preferred_element_type=jnp.float32).astype(
        jnp.bfloat16
    )


def rebuild(latent_out, value_up):
    head_count = value_up.shape[1] // HEAD
    u_parts = value_up.reshape(RANK, head_count, HEAD)
    rebuilt = jnp.einsum("hnr,rhd->nhd", latent_out, u_parts, preferred_element_type=jnp.float32)
    return rebuilt.astype(jnp.bfloat16).reshape(latent_out.shape[1], head_count * HEAD)


def fresh_state(row_shape):
    return (
        jnp.full(row_shape, NEG, jnp.float32),
        jnp.zeros(row_shape, jnp.float32),
        jnp.zeros(row_shape + (RANK,), jnp.float32),
    )


def online(running, scores, key_mask, weigh_fn):
    old_peak, old_total, old_sum = running
    scores = jnp.where(key_mask, scores, NEG)
    new_peak = jnp.maximum(old_peak, jnp.max(scores, axis=-1))
    factor = jnp.exp(old_peak - new_peak)
    weights = jnp.where(key_mask, jnp.exp(scores - new_peak[..., None]), 0.0)
    new_total = old_total * factor + jnp.sum(weights, axis=-1)
    new_sum = old_sum * factor[..., None] + weigh_fn(weights.astype(jnp.bfloat16))
    return (new_peak, new_total, new_sum)


def combine_parts(earlier, second):
    joined_peak = jnp.maximum(earlier[0], second[0])
    left_scale = jnp.exp(earlier[0] - joined_peak)
    right_scale = jnp.exp(second[0] - joined_peak)
    joined_total = earlier[1] * left_scale + second[1] * right_scale
    joined_sum = earlier[2] * left_scale[..., None] + second[2] * right_scale[..., None]
    return (joined_peak, joined_total, joined_sum)


def context_step(running, shard_rows, query_pos, queries_abs, block_order):
    row_count = shard_rows.shape[1]
    key_pos = row_positions(block_order, jnp.arange(row_count, dtype=jnp.int32))
    score_scale = HEAD ** (-0.5)
    for block_start in range(0, row_count, 1024):
        block_end = min(row_count, block_start + 1024)
        key_block = shard_rows[:, block_start:block_end, :RANK]
        value_block = shard_rows[:, block_start:block_end, RANK:]
        key_mask = key_pos[block_start:block_end][None, :] <= query_pos[:, None]
        scores = (
            jnp.einsum("hpnr,pmr->hpnm", queries_abs, key_block, preferred_element_type=jnp.float32)
            * score_scale
        )

        def weigh_block(weights, value_block=value_block):
            return jnp.einsum(
                "hpnm,pmr->hpnr", weights, value_block, preferred_element_type=jnp.float32
            )

        running = online(running, scores, key_mask, weigh_block)
    return running


def local(
    prompt_states,
    prompt_queries,
    decode_states,
    decode_queries,
    latent_down,
    key_up,
    value_up,
    prompt_lengths,
    block_order,
    page_owner,
    decode_context,
):
    prompt_count, prompt_rows, model_width = prompt_states.shape
    cycle_index = lax.axis_index("cp")
    cycle_size = lax.axis_size("cp")
    head_count = key_up.shape[1] // HEAD
    lat_half = jnp.dot(
        prompt_states.reshape(prompt_count * prompt_rows, model_width),
        latent_down,
        preferred_element_type=jnp.float32,
    )
    lat_half = lat_half.astype(jnp.bfloat16).reshape(prompt_count, prompt_rows, RANK)
    new_half = jnp.dot(
        decode_states.reshape(STEPS * ROW_GRP, model_width),
        latent_down,
        preferred_element_type=jnp.float32,
    )
    new_half = new_half.astype(jnp.bfloat16).reshape(STEPS, ROW_GRP, RANK)
    latent, new_latent = (
        lax.all_gather(lat_half, "sec", axis=2, tiled=True),
        lax.all_gather(new_half, "sec", axis=2, tiled=True),
    )
    query_pos = row_positions(
        block_order, cycle_index * prompt_rows + jnp.arange(prompt_rows, dtype=jnp.int32)
    )
    queries_abs = absorb(prompt_queries.reshape(prompt_count * prompt_rows, -1), key_up).reshape(
        head_count, prompt_count, prompt_rows, RANK
    )
    start_state = fresh_state((head_count, prompt_count, prompt_rows))
    owners = page_owner[0]
    slot_ids = jnp.arange(PAGES_DEV, dtype=jnp.int32)
    shard_rows = lax.all_gather(latent, "cp", axis=1, tiled=True)
    running = start_state
    running = context_step(running, shard_rows, query_pos, queries_abs, block_order)
    running, whole_store = (running, shard_rows)
    slot_cap = max(1, PAGES_DEV // cycle_size)
    my_owners = lax.dynamic_index_in_dim(owners, cycle_index, 0, keepdims=False)
    same_owner = (my_owners[:, None] == my_owners[None, :]) & (
        slot_ids[None, :] < slot_ids[:, None]
    )
    send_slot = my_owners * slot_cap + jnp.sum(same_owner.astype(jnp.int32), axis=1)
    select = (
        send_slot[None, :] == jnp.arange(cycle_size * slot_cap, dtype=jnp.int32)[:, None]
    ).astype(jnp.bfloat16)
    page_rows = latent.reshape(PAGES_DEV, PAGE * 2 * RANK)
    outgoing = jnp.dot(select, page_rows, preferred_element_type=jnp.float32).astype(jnp.bfloat16)
    outgoing = outgoing.reshape(cycle_size, slot_cap * PAGE, 2 * RANK)
    incoming = lax.all_to_all(outgoing, "cp", split_axis=0, concat_axis=0, tiled=True)
    counts = jnp.sum((owners == cycle_index).astype(jnp.int32), axis=1)
    source_ids = jnp.arange(counts.shape[0], dtype=jnp.int32)
    offsets = jnp.sum(
        jnp.where(source_ids[None, :] < source_ids[:, None], counts[None, :], 0), axis=1
    )
    places = jnp.arange(slot_cap, dtype=jnp.int32)
    slot_valid = places[None, :] < counts[:, None]
    target = jnp.where(slot_valid, offsets[:, None] + places[None, :], -1).reshape(-1)
    compact = (target[None, :] == slot_ids[:, None]).astype(jnp.bfloat16)
    page_store = jnp.dot(
        compact,
        incoming.reshape(cycle_size * slot_cap, PAGE * 2 * RANK),
        preferred_element_type=jnp.float32,
    )
    page_store = page_store.astype(jnp.bfloat16).reshape(PAGES_DEV * PAGE, 2 * RANK)
    final_peak, final_total, final_sum = running
    prefill_latent = (
        (final_sum / final_total[..., None])
        .astype(jnp.bfloat16)
        .reshape(head_count, prompt_count * prompt_rows, RANK)
    )
    prefill_rows = rebuild(prefill_latent, value_up).reshape(
        prompt_count, prompt_rows, head_count * HEAD
    )
    live_rows = query_pos[None, :] < prompt_lengths[:, None]
    prefill_out = jnp.where(live_rows[..., None], prefill_rows, jnp.zeros_like(prefill_rows))
    rows_all = STEPS * ROW_GRP
    score_scale = HEAD ** (-0.5)
    decode_abs = absorb(decode_queries.reshape(rows_all, -1), key_up)
    row_prompt = jnp.arange(ROW_GRP, dtype=jnp.int32) // (ROW_GRP // PPG)
    row_limit = jnp.minimum(decode_context, lookup(prompt_lengths, row_prompt))
    step_abs = decode_abs.reshape(head_count, STEPS, ROW_GRP, RANK)
    own_scores = (
        jnp.einsum(
            "htnr,snr->htns", step_abs, new_latent[..., :RANK], preferred_element_type=jnp.float32
        )
        * score_scale
    )
    step_ids = jnp.arange(STEPS, dtype=jnp.int32)
    own_mask = (step_ids[None, :] <= step_ids[:, None])[:, None, :]
    own_values = new_latent[..., RANK:]

    def weigh_own(weights):
        return jnp.einsum("htns,snr->htnr", weights, own_values, preferred_element_type=jnp.float32)

    own_part = online(fresh_state((head_count, STEPS, ROW_GRP)), own_scores, own_mask, weigh_own)
    own_part = (
        own_part[0].reshape(head_count, rows_all),
        own_part[1].reshape(head_count, rows_all),
        own_part[2].reshape(head_count, rows_all, RANK),
    )
    share_rows = rows_all // cycle_size
    share_start = cycle_index * share_rows
    share_abs = lax.dynamic_slice_in_dim(decode_abs, share_start, share_rows, 1)
    share_ids = (share_start + jnp.arange(share_rows, dtype=jnp.int32)) % ROW_GRP
    share_prompt = lookup(row_prompt, share_ids)
    share_limit = lookup(row_limit, share_ids)
    whole_rows = whole_store.shape[1]
    whole_pos = row_positions(block_order, jnp.arange(whole_rows, dtype=jnp.int32))
    key_prompt = jnp.broadcast_to(
        jnp.arange(prompt_count, dtype=jnp.int32)[:, None], (prompt_count, whole_rows)
    ).reshape(-1)
    key_pos = jnp.broadcast_to(whole_pos[None, :], (prompt_count, whole_rows)).reshape(-1)
    flat_whole = whole_store.reshape(prompt_count * whole_rows, 2 * RANK)
    whole_mask = (key_prompt[None, :] == share_prompt[:, None]) & (
        key_pos[None, :] < share_limit[:, None]
    )
    whole_scores = (
        jnp.einsum(
            "hqr,mr->hqm", share_abs, flat_whole[:, :RANK], preferred_element_type=jnp.float32
        )
        * score_scale
    )
    whole_values = flat_whole[:, RANK:]

    def weigh_whole(weights):
        return jnp.einsum("hqm,mr->hqr", weights, whole_values, preferred_element_type=jnp.float32)

    whole_part = online(
        fresh_state((head_count, share_rows)), whole_scores, whole_mask, weigh_whole
    )
    own_share = tuple(
        (lax.dynamic_slice_in_dim(member, share_start, share_rows, 1) for member in own_part)
    )
    final_peak, final_total, final_sum = combine_parts(whole_part, own_share)
    decoded = rebuild((final_sum / final_total[..., None]).astype(jnp.bfloat16), value_up)
    decoded = lax.all_gather(decoded, "cp", axis=0, tiled=True)
    decode_out = decoded.reshape(STEPS, ROW_GRP, head_count * HEAD)
    page_cache = page_store.reshape(1, 1, PAGES_DEV * PAGE, 2 * RANK)
    return (prefill_out, decode_out, page_cache)


MESH = pl.DeviceIdType.MESH
KEY_LIMIT = 1024


def gather_kernel(
    n,
    k_chunks,
    states_ref,
    fresh_ref,
    down_ref,
    store_ref,
    new_ref,
    states_buf,
    fresh_buf,
    down_buf,
    load_sem,
    send_sem,
    recv_sem,
    new_send,
    new_recv,
):
    z = lax.axis_index("cp")
    c = lax.axis_index("sec")
    other = 1 - c
    prompts, rows, width = states_ref.shape
    kw = width // k_chunks
    loads = {}
    for k in range(k_chunks):
        cols = pl.ds(k * kw, kw)
        loads["w", k] = pltpu.make_async_copy(
            down_ref.at[cols, :], down_buf.at[cols, :], load_sem.at[0, k]
        )
        loads["w", k].start()
        loads[0, k] = pltpu.make_async_copy(
            states_ref.at[0, :, cols], states_buf.at[0, :, cols], load_sem.at[1, k]
        )
        loads[0, k].start()
    for p in range(1, prompts):
        loads[p, 0] = pltpu.make_async_copy(
            states_ref.at[p], states_buf.at[p], load_sem.at[1 + p, 0]
        )
        loads[p, 0].start()
    loads["d", 0] = pltpu.make_async_copy(fresh_ref, fresh_buf, load_sem.at[1 + prompts, 0])
    loads["d", 0].start()

    def far(gap):
        return gap >= 3

    barrier = pltpu.get_barrier_semaphore()
    pl.semaphore_signal(barrier, inc=1, device_id={"sec": other}, device_id_type=MESH)
    peers = jnp.int32(1)
    for gap in [1] + [g for g in range(1, n) if far(g)]:

        @pl.when(z - gap >= 0)
        def _():
            pl.semaphore_signal(barrier, inc=1, device_id={"cp": z - gap}, device_id_type=MESH)

        @pl.when(z + gap < n)
        def _():
            pl.semaphore_signal(barrier, inc=1, device_id={"cp": z + gap}, device_id_type=MESH)

        peers = peers + (z >= gap).astype(jnp.int32) + (z + gap < n).astype(jnp.int32)

    def piece(half, shard, p):
        return store_ref.at[half, pl.ds((shard * prompts + p) * rows, rows), :]

    def transfer(half, shard, p, way, index, target):
        return pltpu.make_async_remote_copy(
            src_ref=piece(half, shard, p),
            dst_ref=piece(half, shard, p),
            send_sem=send_sem.at[way, index, p],
            recv_sem=recv_sem.at[half, shard, p],
            device_id=target,
            device_id_type=MESH,
        )

    def rightward(shard, p):
        return transfer(c, shard, p, 0, shard, {"cp": z + 1})

    def leftward(shard, p):
        return transfer(c, shard, p, 1, shard, {"cp": z - 1})

    def across(shard, p):
        return transfer(c, shard, p, 2, shard, {"sec": other})

    def direct(target, p):
        return transfer(c, z, p, 3, target, {"cp": target})

    def arrival(shard, p):
        return transfer(c, shard, p, 0, shard, {"cp": z})

    def project(kind, buf):
        chunks = k_chunks if kind == 0 else 1
        step = width // chunks
        total = jnp.zeros((buf.shape[0], down_ref.shape[1]), jnp.float32)
        for k in range(chunks):
            if kind == 0:
                loads["w", k].wait()
            loads[kind, k].wait()
            cols = pl.ds(k * step, step)
            total += jnp.dot(
                buf[:, cols], down_buf[cols, :], preferred_element_type=jnp.float32
            )
        return total.astype(jnp.bfloat16)

    for p in range(prompts):
        store_ref[c, pl.ds((z * prompts + p) * rows, rows), :] = project(p, states_buf.at[p])
        if p == 0:
            pl.semaphore_wait(barrier, peers)

        @pl.when(z > 0)
        def _():
            leftward(z, p).start()

        @pl.when(z < n - 1)
        def _():
            rightward(z, p).start()

        across(z, p).start()
        for gap in range(3, n):

            @pl.when(z - gap >= 0)
            def _():
                direct(z - gap, p).start()

            @pl.when(z + gap < n)
            def _():
                direct(z + gap, p).start()

    new_ref[c] = project("d", fresh_buf)
    new_copy = pltpu.make_async_remote_copy(
        src_ref=new_ref.at[c],
        dst_ref=new_ref.at[c],
        send_sem=new_send,
        recv_sem=new_recv,
        device_id={"sec": other},
        device_id_type=MESH,
    )
    new_copy.start()

    for gap in range(1, n):
        for p in range(prompts):

            @pl.when(z - gap >= 0)
            def _():
                arrival(z - gap, p).wait_recv()
                if gap == 1:

                    @pl.when(z < n - 1)
                    def _():
                        rightward(z - gap, p).start()

                across(z - gap, p).start()

            @pl.when(z + gap < n)
            def _():
                arrival(z + gap, p).wait_recv()
                if gap == 1:

                    @pl.when(z > 0)
                    def _():
                        leftward(z + gap, p).start()

                across(z + gap, p).start()

    for shard in range(n):
        for p in range(prompts):
            transfer(other, shard, p, 2, shard, {"sec": other}).wait_recv()
            across(shard, p).wait_send()

            @pl.when((shard <= z) & (shard >= z - 1) & (z < n - 1))
            def _():
                rightward(shard, p).wait_send()

            @pl.when((shard >= z) & (shard <= z + 1) & (z > 0))
            def _():
                leftward(shard, p).wait_send()

            @pl.when((shard >= z + 3) | (shard <= z - 3))
            def _():
                direct(shard, p).wait_send()

    new_copy.wait_send()
    new_copy.wait_recv()


def gather_latents(n, prompt_states, fresh_states, latent_down):
    prompts, rows, width = prompt_states.shape
    fresh_rows = fresh_states.shape[0]
    k_chunks = 4
    hbm = pl.BlockSpec(memory_space=pltpu.HBM)
    vmem = pl.BlockSpec(memory_space=pltpu.VMEM)
    operands = [
        pltpu.with_memory_space_constraint(array, pltpu.HBM)
        for array in (prompt_states, fresh_states, latent_down)
    ]
    return pl.pallas_call(
        functools.partial(gather_kernel, n, k_chunks),
        out_shape=(
            pltpu.VMEM((2, n * prompts * rows, RANK), jnp.bfloat16),
            pltpu.VMEM((2, fresh_rows, RANK), jnp.bfloat16),
        ),
        in_specs=[hbm] * 3,
        out_specs=(vmem, vmem),
        scratch_shapes=[
            pltpu.VMEM((prompts, rows, width), jnp.bfloat16),
            pltpu.VMEM((fresh_rows, width), jnp.bfloat16),
            pltpu.VMEM(latent_down.shape, jnp.bfloat16),
            pltpu.SemaphoreType.DMA((2 + prompts, k_chunks)),
            pltpu.SemaphoreType.DMA((4, n, prompts)),
            pltpu.SemaphoreType.DMA((2, n, prompts)),
            pltpu.SemaphoreType.DMA,
            pltpu.SemaphoreType.DMA,
        ],
        compiler_params=pltpu.CompilerParams(
            collective_id=0, has_side_effects=True, vmem_limit_bytes=32 * 1024 * 1024
        ),
        name="gather_latents",
    )(*operands)


def attend_kernel(
    n,
    lengths_ref,
    order_ref,
    owner_ref,
    context_ref,
    store_ref,
    new_ref,
    queries_ref,
    fresh_ref,
    key_up_ref,
    value_up_ref,
    prefill_ref,
    decode_ref,
    page_ref,
    pick_ref,
):
    z = lax.axis_index("cp")
    prompts, rows, _ = queries_ref.shape
    heads = key_up_ref.shape[1] // HEAD
    steps, row_grp, _ = fresh_ref.shape
    share = row_grp // prompts
    keys = n * rows
    blocks = rows // BLOCK
    factor = HEAD**-0.5 * math.log2(math.e)
    nt = (((1,), (1,)), ((), ()))
    tn = (((0,), (0,)), ((), ()))
    together = heads

    def stacked(parts):
        return jnp.concatenate(parts, axis=0)

    count = jnp.int32(0)
    pages_dev = owner_ref.shape[2]
    for s in range(n):
        for k in range(pages_dev):
            pick_ref[count] = s * pages_dev + k
            count = count + (owner_ref[0, s, k] == z).astype(jnp.int32)
    for slot in range(pages_dev):
        page = pl.ds(pl.multiple_of(pick_ref[slot] * PAGE, PAGE), PAGE)
        page_ref[0, 0, pl.ds(slot * PAGE, PAGE), :RANK] = store_ref[0, page, :]
        page_ref[0, 0, pl.ds(slot * PAGE, PAGE), RANK:] = store_ref[1, page, :]

    key_pos = stacked(
        [
            lax.broadcasted_iota(jnp.int32, (BLOCK, 1), 0) + order_ref[b] * BLOCK
            for b in range(n * blocks)
        ]
    )
    row = lax.broadcasted_iota(jnp.int32, (rows, 1), 0)
    lane = lax.broadcasted_iota(jnp.int32, (1, together * rows), 1)
    lane = lane % rows
    query_pos = jnp.zeros((rows, 1), jnp.int32)
    asked_pos = jnp.zeros((1, together * rows), jnp.int32)
    for b in range(blocks):
        shift = (order_ref[z * blocks + b] - b) * BLOCK
        query_pos = jnp.where(row // BLOCK == b, row + shift, query_pos)
        asked_pos = jnp.where(lane // BLOCK == b, lane + shift, asked_pos)

    def head_cols(h):
        return pl.ds(h * HEAD, HEAD)

    def absorb_head(rows_in, h):
        return lax.dot_general(
            rows_in, key_up_ref[:, head_cols(h)], nt, preferred_element_type=jnp.float32
        ).astype(jnp.bfloat16)

    def rebuild_head(rows_in, h):
        return jnp.dot(
            rows_in, value_up_ref[:, head_cols(h)], preferred_element_type=jnp.float32
        ).astype(jnp.bfloat16)

    for p in range(prompts):
        pieces = [pl.ds((s * prompts + p) * rows, rows) for s in range(n)]
        key_rows = stacked([store_ref[0, at, :] for at in pieces])
        value_rows = stacked([store_ref[1, at, :] for at in pieces])
        live = query_pos < lengths_ref[p]
        for first in range(0, heads, together):
            group = range(first, first + together)
            absorbed = stacked([absorb_head(queries_ref[p, :, head_cols(h)], h) for h in group])
            scores = lax.dot_general(
                key_rows, absorbed, nt, preferred_element_type=jnp.float32
            )
            scores = jnp.where(key_pos <= asked_pos, scores, NEG)
            peak = jnp.max(scores, axis=0, keepdims=True)
            weights = jnp.exp2((scores - peak) * factor)
            total = jnp.sum(weights, axis=0, keepdims=True)
            summed = lax.dot_general(
                value_rows, weights.astype(jnp.bfloat16), tn, preferred_element_type=jnp.float32
            )
            latent_out = (summed / total).T.astype(jnp.bfloat16)
            for h in group:
                rebuilt = rebuild_head(
                    latent_out[(h - first) * rows : (h - first + 1) * rows], h
                )
                prefill_ref[p, :, head_cols(h)] = jnp.where(
                    live, rebuilt, jnp.zeros_like(rebuilt)
                )

        spot = lax.broadcasted_iota(jnp.int32, (1, heads * steps * share), 1)
        limit = jnp.zeros((1, heads * steps * share), jnp.int32)
        for r in range(share):
            limit = jnp.where(
                spot % share == r,
                jnp.minimum(context_ref[p * share + r], lengths_ref[p]),
                limit,
            )
        mine = [pl.ds(t * row_grp + p * share, share) for t in range(steps)]
        step_rows = steps * share
        step_of = spot // share % steps
        absorbed = stacked(
            [
                absorb_head(
                    stacked(
                        [fresh_ref[t, pl.ds(p * share, share), head_cols(h)] for t in range(steps)]
                    ),
                    h,
                )
                for h in range(heads)
            ]
        )
        scores = lax.dot_general(key_rows, absorbed, nt, preferred_element_type=jnp.float32)
        scores = jnp.where(key_pos < limit, scores, NEG)
        peak = jnp.max(scores, axis=0, keepdims=True)
        wide = absorbed.astype(jnp.float32).T
        own_scores = []
        for t in range(steps):
            own_key = stacked([new_ref[0, mine[t], :].astype(jnp.float32)] * (heads * steps)).T
            own = jnp.sum(wide * own_key, axis=0, keepdims=True)
            own = jnp.where(step_of >= t, own, NEG)
            own_scores.append(own)
            peak = jnp.maximum(peak, own)
        weights = jnp.exp2((scores - peak) * factor)
        total = jnp.sum(weights, axis=0, keepdims=True)
        summed = lax.dot_general(
            value_rows, weights.astype(jnp.bfloat16), tn, preferred_element_type=jnp.float32
        )
        for t in range(steps):
            own_weight = jnp.exp2((own_scores[t] - peak) * factor)
            total = total + own_weight
            own_value = stacked([new_ref[1, mine[t], :].astype(jnp.float32)] * (heads * steps)).T
            summed = summed + own_weight.astype(jnp.bfloat16).astype(jnp.float32) * own_value
        latent_out = (summed / total).T.astype(jnp.bfloat16)
        for h in range(heads):
            rebuilt = rebuild_head(latent_out[h * step_rows : (h + 1) * step_rows], h)
            for t in range(steps):
                decode_ref[t, pl.ds(p * share, share), head_cols(h)] = rebuilt[
                    t * share : (t + 1) * share
                ]


def local_small(
    n,
    prompt_states,
    prompt_queries,
    decode_states,
    decode_queries,
    latent_down,
    key_up,
    value_up,
    prompt_lengths,
    block_order,
    page_owner,
    decode_context,
):
    steps, row_grp, width = decode_states.shape
    store, fresh = gather_latents(
        n, prompt_states, decode_states.reshape(steps * row_grp, width), latent_down
    )
    smem = pl.BlockSpec(memory_space=pltpu.SMEM)
    vmem = pl.BlockSpec(memory_space=pltpu.VMEM)
    pages_dev = page_owner.shape[2]
    return pl.pallas_call(
        functools.partial(attend_kernel, n),
        out_shape=(
            jax.ShapeDtypeStruct(prompt_queries.shape, jnp.bfloat16),
            jax.ShapeDtypeStruct(decode_queries.shape, jnp.bfloat16),
            jax.ShapeDtypeStruct((1, 1, pages_dev * PAGE, 2 * RANK), jnp.bfloat16),
        ),
        in_specs=[smem] * 4 + [vmem] * 6,
        out_specs=(vmem, vmem, vmem),
        scratch_shapes=[pltpu.SMEM((n * pages_dev + 1,), jnp.int32)],
        compiler_params=pltpu.CompilerParams(vmem_limit_bytes=24 * 1024 * 1024),
        name="attend",
    )(
        prompt_lengths,
        block_order,
        page_owner,
        decode_context,
        store,
        fresh,
        prompt_queries,
        decode_queries,
        key_up,
        value_up,
    )


def solution(mesh):
    placed = (
        P("grp", "cp", None),
        P("grp", "cp", "sec"),
        P(None, "grp", None),
        P(None, "grp", "sec"),
        P(None, "sec"),
        P(None, "sec"),
        P(None, "sec"),
        P("grp"),
        P(),
        P("grp", None, None),
        P("grp"),
    )
    n = mesh.shape["cp"]

    def on_device(prompt_states, *others):
        if n * prompt_states.shape[1] <= KEY_LIMIT and mesh.shape["sec"] == 2:
            return local_small(n, prompt_states, *others)
        return local(prompt_states, *others)

    return jax.shard_map(
        on_device,
        mesh=mesh,
        in_specs=placed,
        out_specs=(P("grp", "cp", "sec"), P(None, "grp", "sec"), P("grp", "cp", None, None)),
        check_vma=False,
    )
```

```python
import functools
import math

import jax
import jax.numpy as jnp
from jax import lax
from jax.experimental import pallas as pl
from jax.experimental.pallas import tpu as pltpu
from jax.sharding import PartitionSpec as P

HEAD = 128
RANK = 128
BLOCK = 96
PAGE = 16
PPG = 2
ROW_GRP = 32
STEPS = 3
PAGES_DEV = 24


NEG = -1e30


def lookup(table_rows, indices):
    matches = indices[..., None] == jnp.arange(table_rows.shape[0], dtype=jnp.int32)
    return jnp.sum(jnp.where(matches, table_rows, 0), axis=-1)


def row_positions(block_order, stored_rows):
    return lookup(block_order, stored_rows // BLOCK) * BLOCK + stored_rows % BLOCK


def absorb(queries, key_up):
    row_count = queries.shape[0]
    head_count = key_up.shape[1] // HEAD
    q_parts = queries.reshape(row_count, head_count, HEAD)
    u_parts = key_up.reshape(RANK, head_count, HEAD)
    return jnp.einsum("nhd,rhd->hnr", q_parts, u_parts, preferred_element_type=jnp.float32).astype(
        jnp.bfloat16
    )


def rebuild(latent_out, value_up):
    head_count = value_up.shape[1] // HEAD
    u_parts = value_up.reshape(RANK, head_count, HEAD)
    rebuilt = jnp.einsum("hnr,rhd->nhd", latent_out, u_parts, preferred_element_type=jnp.float32)
    return rebuilt.astype(jnp.bfloat16).reshape(latent_out.shape[1], head_count * HEAD)


def fresh_state(row_shape):
    return (
        jnp.full(row_shape, NEG, jnp.float32),
        jnp.zeros(row_shape, jnp.float32),
        jnp.zeros(row_shape + (RANK,), jnp.float32),
    )


def online(running, scores, key_mask, weigh_fn):
    old_peak, old_total, old_sum = running
    scores = jnp.where(key_mask, scores, NEG)
    new_peak = jnp.maximum(old_peak, jnp.max(scores, axis=-1))
    factor = jnp.exp(old_peak - new_peak)
    weights = jnp.where(key_mask, jnp.exp(scores - new_peak[..., None]), 0.0)
    new_total = old_total * factor + jnp.sum(weights, axis=-1)
    new_sum = old_sum * factor[..., None] + weigh_fn(weights.astype(jnp.bfloat16))
    return (new_peak, new_total, new_sum)


def combine_parts(earlier, second):
    joined_peak = jnp.maximum(earlier[0], second[0])
    left_scale = jnp.exp(earlier[0] - joined_peak)
    right_scale = jnp.exp(second[0] - joined_peak)
    joined_total = earlier[1] * left_scale + second[1] * right_scale
    joined_sum = earlier[2] * left_scale[..., None] + second[2] * right_scale[..., None]
    return (joined_peak, joined_total, joined_sum)


def context_step(running, shard_rows, query_pos, queries_abs, block_order):
    row_count = shard_rows.shape[1]
    key_pos = row_positions(block_order, jnp.arange(row_count, dtype=jnp.int32))
    score_scale = HEAD ** (-0.5)
    for block_start in range(0, row_count, 1024):
        block_end = min(row_count, block_start + 1024)
        key_block = shard_rows[:, block_start:block_end, :RANK]
        value_block = shard_rows[:, block_start:block_end, RANK:]
        key_mask = key_pos[block_start:block_end][None, :] <= query_pos[:, None]
        scores = (
            jnp.einsum("hpnr,pmr->hpnm", queries_abs, key_block, preferred_element_type=jnp.float32)
            * score_scale
        )

        def weigh_block(weights, value_block=value_block):
            return jnp.einsum(
                "hpnm,pmr->hpnr", weights, value_block, preferred_element_type=jnp.float32
            )

        running = online(running, scores, key_mask, weigh_block)
    return running


def local(
    prompt_states,
    prompt_queries,
    decode_states,
    decode_queries,
    latent_down,
    key_up,
    value_up,
    prompt_lengths,
    block_order,
    page_owner,
    decode_context,
):
    prompt_count, prompt_rows, model_width = prompt_states.shape
    cycle_index = lax.axis_index("cp")
    cycle_size = lax.axis_size("cp")
    head_count = key_up.shape[1] // HEAD
    lat_half = jnp.dot(
        prompt_states.reshape(prompt_count * prompt_rows, model_width),
        latent_down,
        preferred_element_type=jnp.float32,
    )
    lat_half = lat_half.astype(jnp.bfloat16).reshape(prompt_count, prompt_rows, RANK)
    new_half = jnp.dot(
        decode_states.reshape(STEPS * ROW_GRP, model_width),
        latent_down,
        preferred_element_type=jnp.float32,
    )
    new_half = new_half.astype(jnp.bfloat16).reshape(STEPS, ROW_GRP, RANK)
    latent, new_latent = (
        lax.all_gather(lat_half, "sec", axis=2, tiled=True),
        lax.all_gather(new_half, "sec", axis=2, tiled=True),
    )
    query_pos = row_positions(
        block_order, cycle_index * prompt_rows + jnp.arange(prompt_rows, dtype=jnp.int32)
    )
    queries_abs = absorb(prompt_queries.reshape(prompt_count * prompt_rows, -1), key_up).reshape(
        head_count, prompt_count, prompt_rows, RANK
    )
    start_state = fresh_state((head_count, prompt_count, prompt_rows))
    owners = page_owner[0]
    slot_ids = jnp.arange(PAGES_DEV, dtype=jnp.int32)
    shard_rows = lax.all_gather(latent, "cp", axis=1, tiled=True)
    running = start_state
    running = context_step(running, shard_rows, query_pos, queries_abs, block_order)
    running, whole_store = (running, shard_rows)
    slot_cap = max(1, PAGES_DEV // cycle_size)
    my_owners = lax.dynamic_index_in_dim(owners, cycle_index, 0, keepdims=False)
    same_owner = (my_owners[:, None] == my_owners[None, :]) & (
        slot_ids[None, :] < slot_ids[:, None]
    )
    send_slot = my_owners * slot_cap + jnp.sum(same_owner.astype(jnp.int32), axis=1)
    select = (
        send_slot[None, :] == jnp.arange(cycle_size * slot_cap, dtype=jnp.int32)[:, None]
    ).astype(jnp.bfloat16)
    page_rows = latent.reshape(PAGES_DEV, PAGE * 2 * RANK)
    outgoing = jnp.dot(select, page_rows, preferred_element_type=jnp.float32).astype(jnp.bfloat16)
    outgoing = outgoing.reshape(cycle_size, slot_cap * PAGE, 2 * RANK)
    incoming = lax.all_to_all(outgoing, "cp", split_axis=0, concat_axis=0, tiled=True)
    counts = jnp.sum((owners == cycle_index).astype(jnp.int32), axis=1)
    source_ids = jnp.arange(counts.shape[0], dtype=jnp.int32)
    offsets = jnp.sum(
        jnp.where(source_ids[None, :] < source_ids[:, None], counts[None, :], 0), axis=1
    )
    places = jnp.arange(slot_cap, dtype=jnp.int32)
    slot_valid = places[None, :] < counts[:, None]
    target = jnp.where(slot_valid, offsets[:, None] + places[None, :], -1).reshape(-1)
    compact = (target[None, :] == slot_ids[:, None]).astype(jnp.bfloat16)
    page_store = jnp.dot(
        compact,
        incoming.reshape(cycle_size * slot_cap, PAGE * 2 * RANK),
        preferred_element_type=jnp.float32,
    )
    page_store = page_store.astype(jnp.bfloat16).reshape(PAGES_DEV * PAGE, 2 * RANK)
    final_peak, final_total, final_sum = running
    prefill_latent = (
        (final_sum / final_total[..., None])
        .astype(jnp.bfloat16)
        .reshape(head_count, prompt_count * prompt_rows, RANK)
    )
    prefill_rows = rebuild(prefill_latent, value_up).reshape(
        prompt_count, prompt_rows, head_count * HEAD
    )
    live_rows = query_pos[None, :] < prompt_lengths[:, None]
    prefill_out = jnp.where(live_rows[..., None], prefill_rows, jnp.zeros_like(prefill_rows))
    rows_all = STEPS * ROW_GRP
    score_scale = HEAD ** (-0.5)
    decode_abs = absorb(decode_queries.reshape(rows_all, -1), key_up)
    row_prompt = jnp.arange(ROW_GRP, dtype=jnp.int32) // (ROW_GRP // PPG)
    row_limit = jnp.minimum(decode_context, lookup(prompt_lengths, row_prompt))
    step_abs = decode_abs.reshape(head_count, STEPS, ROW_GRP, RANK)
    own_scores = (
        jnp.einsum(
            "htnr,snr->htns", step_abs, new_latent[..., :RANK], preferred_element_type=jnp.float32
        )
        * score_scale
    )
    step_ids = jnp.arange(STEPS, dtype=jnp.int32)
    own_mask = (step_ids[None, :] <= step_ids[:, None])[:, None, :]
    own_values = new_latent[..., RANK:]

    def weigh_own(weights):
        return jnp.einsum("htns,snr->htnr", weights, own_values, preferred_element_type=jnp.float32)

    own_part = online(fresh_state((head_count, STEPS, ROW_GRP)), own_scores, own_mask, weigh_own)
    own_part = (
        own_part[0].reshape(head_count, rows_all),
        own_part[1].reshape(head_count, rows_all),
        own_part[2].reshape(head_count, rows_all, RANK),
    )
    share_rows = rows_all // cycle_size
    share_start = cycle_index * share_rows
    share_abs = lax.dynamic_slice_in_dim(decode_abs, share_start, share_rows, 1)
    share_ids = (share_start + jnp.arange(share_rows, dtype=jnp.int32)) % ROW_GRP
    share_prompt = lookup(row_prompt, share_ids)
    share_limit = lookup(row_limit, share_ids)
    whole_rows = whole_store.shape[1]
    whole_pos = row_positions(block_order, jnp.arange(whole_rows, dtype=jnp.int32))
    key_prompt = jnp.broadcast_to(
        jnp.arange(prompt_count, dtype=jnp.int32)[:, None], (prompt_count, whole_rows)
    ).reshape(-1)
    key_pos = jnp.broadcast_to(whole_pos[None, :], (prompt_count, whole_rows)).reshape(-1)
    flat_whole = whole_store.reshape(prompt_count * whole_rows, 2 * RANK)
    whole_mask = (key_prompt[None, :] == share_prompt[:, None]) & (
        key_pos[None, :] < share_limit[:, None]
    )
    whole_scores = (
        jnp.einsum(
            "hqr,mr->hqm", share_abs, flat_whole[:, :RANK], preferred_element_type=jnp.float32
        )
        * score_scale
    )
    whole_values = flat_whole[:, RANK:]

    def weigh_whole(weights):
        return jnp.einsum("hqm,mr->hqr", weights, whole_values, preferred_element_type=jnp.float32)

    whole_part = online(
        fresh_state((head_count, share_rows)), whole_scores, whole_mask, weigh_whole
    )
    own_share = tuple(
        (lax.dynamic_slice_in_dim(member, share_start, share_rows, 1) for member in own_part)
    )
    final_peak, final_total, final_sum = combine_parts(whole_part, own_share)
    decoded = rebuild((final_sum / final_total[..., None]).astype(jnp.bfloat16), value_up)
    decoded = lax.all_gather(decoded, "cp", axis=0, tiled=True)
    decode_out = decoded.reshape(STEPS, ROW_GRP, head_count * HEAD)
    page_cache = page_store.reshape(1, 1, PAGES_DEV * PAGE, 2 * RANK)
    return (prefill_out, decode_out, page_cache)


MESH = pl.DeviceIdType.MESH
KEY_LIMIT = 1024


def fused_kernel(
    n,
    k_chunks,
    lengths_hbm,
    order_hbm,
    context_hbm,
    states_hbm,
    fresh_hbm,
    down_hbm,
    queries_hbm,
    asks_hbm,
    key_up_hbm,
    value_up_hbm,
    store_ref,
    prefill_ref,
    decode_ref,
    lengths_ref,
    order_ref,
    context_ref,
    states_buf,
    fresh_buf,
    down_buf,
    queries_ref,
    asks_ref,
    key_up_ref,
    value_up_ref,
    new_ref,
    absorbed_ref,
    asked_ref,
    peak_ref,
    total_ref,
    sum_ref,
    load_sem,
    small_sem,
    send_sem,
    recv_sem,
    new_send,
    new_recv,
):
    z = lax.axis_index("cp")
    c = lax.axis_index("sec")
    other = 1 - c
    prompts, rows, width = states_hbm.shape
    heads = key_up_ref.shape[1] // HEAD
    steps, row_grp, _ = asks_ref.shape
    share = row_grp // prompts
    blocks = rows // BLOCK
    asking = heads * rows
    fresh_lanes = heads * steps * share
    lanes = asking + fresh_lanes
    factor = HEAD**-0.5 * math.log2(math.e)
    nt = (((1,), (1,)), ((), ()))
    tn = (((0,), (0,)), ((), ()))
    kw = width // k_chunks
    later_chunks = 2

    small = [
        pltpu.make_async_copy(source, held, small_sem.at[i])
        for i, (source, held) in enumerate(
            [
                (order_hbm, order_ref),
                (lengths_hbm, lengths_ref),
                (context_hbm, context_ref),
                (key_up_hbm, key_up_ref),
                (queries_hbm, queries_ref),
                (asks_hbm, asks_ref),
                (value_up_hbm, value_up_ref),
            ]
        )
    ]
    loads = {}
    for copy in small[:3]:
        copy.start()
    for k in range(k_chunks):
        cols = pl.ds(k * kw, kw)
        loads["w", k] = pltpu.make_async_copy(
            down_hbm.at[cols, :], down_buf.at[cols, :], load_sem.at[0, k]
        )
        loads["w", k].start()
        loads[0, k] = pltpu.make_async_copy(
            states_hbm.at[0, :, cols], states_buf.at[0, :, cols], load_sem.at[1, k]
        )
        loads[0, k].start()
    for p in range(1, prompts):
        for k in range(later_chunks):
            cols = pl.ds(k * (width // later_chunks), width // later_chunks)
            loads[p, k] = pltpu.make_async_copy(
                states_hbm.at[p, :, cols], states_buf.at[p, :, cols], load_sem.at[1 + p, k]
            )
            loads[p, k].start()
    loads["d", 0] = pltpu.make_async_copy(fresh_hbm, fresh_buf, load_sem.at[1 + prompts, 0])
    loads["d", 0].start()
    for copy in small[3:]:
        copy.start()

    barrier = pltpu.get_barrier_semaphore()
    pl.semaphore_signal(barrier, inc=1, device_id={"sec": other}, device_id_type=MESH)
    peers = jnp.int32(1)
    for gap in [g for g in range(1, n) if g != 2]:

        @pl.when(z - gap >= 0)
        def _():
            pl.semaphore_signal(barrier, inc=1, device_id={"cp": z - gap}, device_id_type=MESH)

        @pl.when(z + gap < n)
        def _():
            pl.semaphore_signal(barrier, inc=1, device_id={"cp": z + gap}, device_id_type=MESH)

        peers = peers + (z >= gap).astype(jnp.int32) + (z + gap < n).astype(jnp.int32)

    def shard_rows(shard, p):
        return pl.ds(pl.multiple_of((shard * prompts + p) * rows, rows), rows)

    def transfer(half, shard, p, way, index, target):
        piece = store_ref.at[half, shard_rows(shard, p), :]
        return pltpu.make_async_remote_copy(
            src_ref=piece,
            dst_ref=piece,
            send_sem=send_sem.at[way, index, p],
            recv_sem=recv_sem.at[half, shard, p],
            device_id=target,
            device_id_type=MESH,
        )

    def rightward(shard, p):
        return transfer(c, shard, p, 0, shard, {"cp": z + 1})

    def leftward(shard, p):
        return transfer(c, shard, p, 1, shard, {"cp": z - 1})

    def across(shard, p):
        return transfer(c, shard, p, 2, shard, {"sec": other})

    def direct(target, p):
        return transfer(c, z, p, 3, target, {"cp": target})

    def arrival(shard, p):
        return transfer(c, shard, p, 0, shard, {"cp": z})

    def wait_other(shard, p):
        transfer(other, shard, p, 2, shard, {"sec": other}).wait_recv()

    def project(kind, buf):
        chunks = {0: k_chunks, "d": 1}.get(kind, later_chunks)
        step = width // chunks
        total = jnp.zeros((buf.shape[0], down_buf.shape[1]), jnp.float32)
        for k in range(chunks):
            if kind == 0:
                loads["w", k].wait()
            loads[kind, k].wait()
            cols = pl.ds(k * step, step)
            total += jnp.dot(
                buf[:, cols], down_buf[cols, :], preferred_element_type=jnp.float32
            )
        return total.astype(jnp.bfloat16)

    def stacked(parts):
        return jnp.concatenate(parts, axis=0)

    def head_cols(h):
        return pl.ds(h * HEAD, HEAD)

    def absorb_head(rows_in, h):
        return lax.dot_general(
            rows_in, key_up_ref[:, head_cols(h)], nt, preferred_element_type=jnp.float32
        ).astype(jnp.bfloat16)

    def rebuild_head(rows_in, h):
        return jnp.dot(
            rows_in, value_up_ref[:, head_cols(h)], preferred_element_type=jnp.float32
        ).astype(jnp.bfloat16)

    def place(shard, column):
        row = lax.broadcasted_iota(jnp.int32, (rows, 1) if column else (1, asking), 1 - column)
        row = row if column else row % rows
        found = jnp.zeros_like(row)
        for b in range(blocks):
            shift = (order_ref[shard * blocks + b] - b) * BLOCK
            found = jnp.where(row // BLOCK == b, row + shift, found)
        return found

    for copy in small[:3]:
        copy.wait()
    asked_rows = place(z, 0)
    spot = lax.broadcasted_iota(jnp.int32, (1, fresh_lanes), 1)
    for p in range(prompts):
        asked_ref[p, :, pl.ds(0, asking)] = asked_rows
        limit = jnp.zeros((1, fresh_lanes), jnp.int32)
        for r in range(share):
            limit = jnp.where(
                spot % share == r,
                jnp.minimum(context_ref[p * share + r], lengths_ref[p]) - 1,
                limit,
            )
        asked_ref[p, :, pl.ds(asking, fresh_lanes)] = limit

    for p in range(prompts):
        store_ref[c, shard_rows(z, p), :] = project(p, states_buf.at[p])
        if p == 0:
            pl.semaphore_wait(barrier, peers)

        @pl.when(z > 0)
        def _():
            leftward(z, p).start()

        @pl.when(z < n - 1)
        def _():
            rightward(z, p).start()

        across(z, p).start()
        for gap in range(3, n):

            @pl.when(z - gap >= 0)
            def _():
                direct(z - gap, p).start()

            @pl.when(z + gap < n)
            def _():
                direct(z + gap, p).start()

    new_ref[c] = project("d", fresh_buf)
    new_copy = pltpu.make_async_remote_copy(
        src_ref=new_ref.at[c],
        dst_ref=new_ref.at[c],
        send_sem=new_send,
        recv_sem=new_recv,
        device_id={"sec": other},
        device_id_type=MESH,
    )
    new_copy.start()

    for copy in small[3:]:
        copy.wait()
    for p in range(prompts):
        for h in range(heads):
            absorbed_ref[p, pl.ds(h * rows, rows), :] = absorb_head(
                queries_ref[p, :, head_cols(h)], h
            )
            asks = stacked([asks_ref[t, pl.ds(p * share, share), head_cols(h)] for t in range(steps)])
            absorbed_ref[p, pl.ds(asking + h * steps * share, steps * share), :] = absorb_head(asks, h)

    fresh_at = pl.ds(asking, fresh_lanes)
    step_of = spot // share % steps

    def attend_own(p):
        mine = [pl.ds(t * row_grp + p * share, share) for t in range(steps)]
        wide = absorbed_ref[p, fresh_at, :].astype(jnp.float32).T
        own_scores = []
        for t in range(steps):
            own_key = stacked([new_ref[0, mine[t], :].astype(jnp.float32)] * (heads * steps)).T
            own = jnp.sum(wide * own_key, axis=0, keepdims=True)
            own_scores.append(jnp.where(step_of >= t, own, NEG))
        old_peak = peak_ref[p, :, fresh_at]
        peak = functools.reduce(jnp.maximum, own_scores, old_peak)
        rescale = jnp.exp2((old_peak - peak) * factor)
        total = total_ref[p, :, fresh_at] * rescale
        summed = sum_ref[p, :, fresh_at] * rescale
        for t in range(steps):
            own_weight = jnp.exp2((own_scores[t] - peak) * factor)
            total = total + own_weight
            own_value = stacked([new_ref[1, mine[t], :].astype(jnp.float32)] * (heads * steps)).T
            summed = summed + own_weight.astype(jnp.bfloat16).astype(jnp.float32) * own_value
        peak_ref[p, :, fresh_at] = peak
        total_ref[p, :, fresh_at] = total
        sum_ref[p, :, fresh_at] = summed

    def attend(shard, p, first=False):
        wait_other(shard, p)
        key_rows = store_ref[0, shard_rows(shard, p), :]
        value_rows = store_ref[1, shard_rows(shard, p), :]
        scores = lax.dot_general(
            key_rows, absorbed_ref[p], nt, preferred_element_type=jnp.float32
        )
        scores = jnp.where(place(shard, 1) <= asked_ref[p], scores, NEG)
        peak = jnp.max(scores, axis=0, keepdims=True)
        if not first:
            old_peak = peak_ref[p]
            peak = jnp.maximum(old_peak, peak)
            rescale = jnp.exp2((old_peak - peak) * factor)
        weights = jnp.exp2((scores - peak) * factor)
        total = jnp.sum(weights, axis=0, keepdims=True)
        summed = lax.dot_general(
            value_rows, weights.astype(jnp.bfloat16), tn, preferred_element_type=jnp.float32
        )
        if not first:
            total = total_ref[p] * rescale + total
            summed = sum_ref[p] * rescale + summed
        peak_ref[p] = peak
        total_ref[p] = total
        sum_ref[p] = summed

    def finish(p):
        latent_out = (sum_ref[p] * (1.0 / total_ref[p])).T.astype(jnp.bfloat16)
        live = place(z, 1) < lengths_ref[p]
        for h in range(heads):
            rebuilt = rebuild_head(latent_out[h * rows : (h + 1) * rows], h)
            prefill_ref[p, :, head_cols(h)] = jnp.where(live, rebuilt, jnp.zeros_like(rebuilt))
            first = asking + h * steps * share
            rebuilt = rebuild_head(latent_out[first : first + steps * share], h)
            for t in range(steps):
                decode_ref[t, pl.ds(p * share, share), head_cols(h)] = rebuilt[
                    t * share : (t + 1) * share
                ]

    def receive(gap, p):
        @pl.when(z - gap >= 0)
        def _():
            arrival(z - gap, p).wait_recv()
            if gap == 1:

                @pl.when(z < n - 1)
                def _():
                    rightward(z - gap, p).start()

            across(z - gap, p).start()

        @pl.when(z + gap < n)
        def _():
            arrival(z + gap, p).wait_recv()
            if gap == 1:

                @pl.when(z > 0)
                def _():
                    leftward(z + gap, p).start()

            across(z + gap, p).start()

    def source(step):
        left, right = z, n - 1 - z
        both = jnp.minimum(left, right)
        near = z - (step + 1) // 2 if step % 2 else z + step // 2
        far = jnp.where(left > right, z - (step - both), z + (step - both))
        return jnp.where(step <= 2 * both, near, far)

    later = [(step, p) for p in range(prompts) for step in range(n - 1, 1, -1)]
    for p in range(prompts):
        attend(z, p, first=True)
        receive(1, p)
    new_copy.wait_recv()
    for p in range(prompts):
        attend_own(p)
    pending = list(later)
    for p in range(prompts):
        attend(source(1), p)
        if pending:
            receive(*pending.pop(0))
    for at, (step, p) in enumerate(later):
        attend(source(step), p)
        if pending:
            receive(*pending.pop(0))
        if at == len(later) - 1 or later[at + 1][1] != p:
            finish(p)

    for shard in range(n):
        for p in range(prompts):
            across(shard, p).wait_send()

            @pl.when((shard <= z) & (shard >= z - 1) & (z < n - 1))
            def _():
                rightward(shard, p).wait_send()

            @pl.when((shard >= z) & (shard <= z + 1) & (z > 0))
            def _():
                leftward(shard, p).wait_send()

            @pl.when((shard >= z + 3) | (shard <= z - 3))
            def _():
                direct(shard, p).wait_send()

    new_copy.wait_send()


def hand_over_kernel(
    n,
    owner_ref,
    store_ref,
    prefill_ref,
    decode_ref,
    prefill_out,
    decode_out,
    page_out,
    pages_ref,
    pick_ref,
    sems,
):
    z = lax.axis_index("cp")
    whole = [
        pltpu.make_async_copy(prefill_ref, prefill_out, sems.at[0]),
        pltpu.make_async_copy(decode_ref, decode_out, sems.at[1]),
    ]
    for copy in whole:
        copy.start()
    count = jnp.int32(0)
    pages_dev = owner_ref.shape[2]
    for s in range(n):
        for k in range(pages_dev):
            pick_ref[count] = s * pages_dev + k
            count = count + (owner_ref[0, s, k] == z).astype(jnp.int32)
    for slot in range(pages_dev):
        page = pl.ds(pl.multiple_of(pick_ref[slot] * PAGE, PAGE), PAGE)
        pages_ref[0, 0, pl.ds(slot * PAGE, PAGE), :RANK] = store_ref[0, page, :]
        pages_ref[0, 0, pl.ds(slot * PAGE, PAGE), RANK:] = store_ref[1, page, :]
    whole.append(pltpu.make_async_copy(pages_ref, page_out, sems.at[2]))
    whole[-1].start()
    for copy in whole:
        copy.wait()


def local_small(
    n,
    prompt_states,
    prompt_queries,
    decode_states,
    decode_queries,
    latent_down,
    key_up,
    value_up,
    prompt_lengths,
    block_order,
    page_owner,
    decode_context,
):
    steps, row_grp, width = decode_states.shape
    prompts, rows, _ = prompt_states.shape
    fresh_rows = steps * row_grp
    heads = key_up.shape[1] // HEAD
    lanes = heads * (rows + steps * (row_grp // prompts))
    k_chunks = 4
    hbm = pl.BlockSpec(memory_space=pltpu.HBM)
    smem = pl.BlockSpec(memory_space=pltpu.SMEM)
    vmem = pl.BlockSpec(memory_space=pltpu.VMEM)
    operands = [
        pltpu.with_memory_space_constraint(array, pltpu.HBM)
        for array in (
            prompt_lengths,
            block_order,
            decode_context,
            prompt_states,
            decode_states.reshape(fresh_rows, width),
            latent_down,
            prompt_queries,
            decode_queries,
            key_up,
            value_up,
        )
    ]
    dma = pltpu.SemaphoreType.DMA
    store, prefill, decoded = pl.pallas_call(
        functools.partial(fused_kernel, n, k_chunks),
        out_shape=(
            pltpu.VMEM((2, n * prompts * rows, RANK), jnp.bfloat16),
            pltpu.VMEM(prompt_queries.shape, jnp.bfloat16),
            pltpu.VMEM(decode_queries.shape, jnp.bfloat16),
        ),
        in_specs=[hbm] * len(operands),
        out_specs=(vmem,) * 3,
        scratch_shapes=[
            pltpu.SMEM(prompt_lengths.shape, jnp.int32),
            pltpu.SMEM(block_order.shape, jnp.int32),
            pltpu.SMEM(decode_context.shape, jnp.int32),
            pltpu.VMEM((prompts, rows, width), jnp.bfloat16),
            pltpu.VMEM((fresh_rows, width), jnp.bfloat16),
            pltpu.VMEM(latent_down.shape, jnp.bfloat16),
            pltpu.VMEM(prompt_queries.shape, jnp.bfloat16),
            pltpu.VMEM(decode_queries.shape, jnp.bfloat16),
            pltpu.VMEM(key_up.shape, jnp.bfloat16),
            pltpu.VMEM(value_up.shape, jnp.bfloat16),
            pltpu.VMEM((2, fresh_rows, RANK), jnp.bfloat16),
            pltpu.VMEM((prompts, lanes, RANK), jnp.bfloat16),
            pltpu.VMEM((prompts, 1, lanes), jnp.int32),
            pltpu.VMEM((prompts, 1, lanes), jnp.float32),
            pltpu.VMEM((prompts, 1, lanes), jnp.float32),
            pltpu.VMEM((prompts, RANK, lanes), jnp.float32),
            dma((2 + prompts, k_chunks)),
            dma((7,)),
            dma((4, n, prompts)),
            dma((2, n, prompts)),
            dma,
            dma,
        ],
        compiler_params=pltpu.CompilerParams(
            collective_id=0, has_side_effects=True, vmem_limit_bytes=40 * 1024 * 1024
        ),
        name="gather_attend",
    )(*operands)
    pages_dev = page_owner.shape[2]
    page_shape = (1, 1, pages_dev * PAGE, 2 * RANK)
    return pl.pallas_call(
        functools.partial(hand_over_kernel, n),
        out_shape=(
            jax.ShapeDtypeStruct(prompt_queries.shape, jnp.bfloat16),
            jax.ShapeDtypeStruct(decode_queries.shape, jnp.bfloat16),
            jax.ShapeDtypeStruct(page_shape, jnp.bfloat16),
        ),
        in_specs=[smem] + [vmem] * 3,
        out_specs=(hbm,) * 3,
        scratch_shapes=[
            pltpu.VMEM(page_shape, jnp.bfloat16),
            pltpu.SMEM((n * pages_dev + 1,), jnp.int32),
            dma((3,)),
        ],
        compiler_params=pltpu.CompilerParams(vmem_limit_bytes=8 * 1024 * 1024),
        name="hand_over",
    )(page_owner, store, prefill, decoded)


def solution(mesh):
    placed = (
        P("grp", "cp", None),
        P("grp", "cp", "sec"),
        P(None, "grp", None),
        P(None, "grp", "sec"),
        P(None, "sec"),
        P(None, "sec"),
        P(None, "sec"),
        P("grp"),
        P(),
        P("grp", None, None),
        P("grp"),
    )
    n = mesh.shape["cp"]

    def on_device(prompt_states, *others):
        if n * prompt_states.shape[1] <= KEY_LIMIT and mesh.shape["sec"] == 2:
            return local_small(n, prompt_states, *others)
        return local(prompt_states, *others)

    return jax.shard_map(
        on_device,
        mesh=mesh,
        in_specs=placed,
        out_specs=(P("grp", "cp", "sec"), P(None, "grp", "sec"), P("grp", "cp", None, None)),
        check_vma=False,
    )
```

```python
import functools
import math

import jax
import jax.numpy as jnp
from jax import lax
from jax.experimental import pallas as pl
from jax.experimental.pallas import tpu as pltpu
from jax.sharding import PartitionSpec as P

HEAD = 128
RANK = 128
BLOCK = 96
PAGE = 16
PPG = 2
ROW_GRP = 32
STEPS = 3
PAGES_DEV = 24


NEG = -1e30


def lookup(table_rows, indices):
    matches = indices[..., None] == jnp.arange(table_rows.shape[0], dtype=jnp.int32)
    return jnp.sum(jnp.where(matches, table_rows, 0), axis=-1)


def row_positions(block_order, stored_rows):
    return lookup(block_order, stored_rows // BLOCK) * BLOCK + stored_rows % BLOCK


def absorb(queries, key_up):
    row_count = queries.shape[0]
    head_count = key_up.shape[1] // HEAD
    q_parts = queries.reshape(row_count, head_count, HEAD)
    u_parts = key_up.reshape(RANK, head_count, HEAD)
    return jnp.einsum("nhd,rhd->hnr", q_parts, u_parts, preferred_element_type=jnp.float32).astype(
        jnp.bfloat16
    )


def rebuild(latent_out, value_up):
    head_count = value_up.shape[1] // HEAD
    u_parts = value_up.reshape(RANK, head_count, HEAD)
    rebuilt = jnp.einsum("hnr,rhd->nhd", latent_out, u_parts, preferred_element_type=jnp.float32)
    return rebuilt.astype(jnp.bfloat16).reshape(latent_out.shape[1], head_count * HEAD)


def fresh_state(row_shape):
    return (
        jnp.full(row_shape, NEG, jnp.float32),
        jnp.zeros(row_shape, jnp.float32),
        jnp.zeros(row_shape + (RANK,), jnp.float32),
    )


def online(running, scores, key_mask, weigh_fn):
    old_peak, old_total, old_sum = running
    scores = jnp.where(key_mask, scores, NEG)
    new_peak = jnp.maximum(old_peak, jnp.max(scores, axis=-1))
    factor = jnp.exp(old_peak - new_peak)
    weights = jnp.where(key_mask, jnp.exp(scores - new_peak[..., None]), 0.0)
    new_total = old_total * factor + jnp.sum(weights, axis=-1)
    new_sum = old_sum * factor[..., None] + weigh_fn(weights.astype(jnp.bfloat16))
    return (new_peak, new_total, new_sum)


def combine_parts(earlier, second):
    joined_peak = jnp.maximum(earlier[0], second[0])
    left_scale = jnp.exp(earlier[0] - joined_peak)
    right_scale = jnp.exp(second[0] - joined_peak)
    joined_total = earlier[1] * left_scale + second[1] * right_scale
    joined_sum = earlier[2] * left_scale[..., None] + second[2] * right_scale[..., None]
    return (joined_peak, joined_total, joined_sum)


def context_step(running, shard_rows, query_pos, queries_abs, block_order):
    row_count = shard_rows.shape[1]
    key_pos = row_positions(block_order, jnp.arange(row_count, dtype=jnp.int32))
    score_scale = HEAD ** (-0.5)
    for block_start in range(0, row_count, 1024):
        block_end = min(row_count, block_start + 1024)
        key_block = shard_rows[:, block_start:block_end, :RANK]
        value_block = shard_rows[:, block_start:block_end, RANK:]
        key_mask = key_pos[block_start:block_end][None, :] <= query_pos[:, None]
        scores = (
            jnp.einsum("hpnr,pmr->hpnm", queries_abs, key_block, preferred_element_type=jnp.float32)
            * score_scale
        )

        def weigh_block(weights, value_block=value_block):
            return jnp.einsum(
                "hpnm,pmr->hpnr", weights, value_block, preferred_element_type=jnp.float32
            )

        running = online(running, scores, key_mask, weigh_block)
    return running


def local(
    prompt_states,
    prompt_queries,
    decode_states,
    decode_queries,
    latent_down,
    key_up,
    value_up,
    prompt_lengths,
    block_order,
    page_owner,
    decode_context,
):
    prompt_count, prompt_rows, model_width = prompt_states.shape
    cycle_index = lax.axis_index("cp")
    cycle_size = lax.axis_size("cp")
    head_count = key_up.shape[1] // HEAD
    lat_half = jnp.dot(
        prompt_states.reshape(prompt_count * prompt_rows, model_width),
        latent_down,
        preferred_element_type=jnp.float32,
    )
    lat_half = lat_half.astype(jnp.bfloat16).reshape(prompt_count, prompt_rows, RANK)
    new_half = jnp.dot(
        decode_states.reshape(STEPS * ROW_GRP, model_width),
        latent_down,
        preferred_element_type=jnp.float32,
    )
    new_half = new_half.astype(jnp.bfloat16).reshape(STEPS, ROW_GRP, RANK)
    latent, new_latent = (
        lax.all_gather(lat_half, "sec", axis=2, tiled=True),
        lax.all_gather(new_half, "sec", axis=2, tiled=True),
    )
    query_pos = row_positions(
        block_order, cycle_index * prompt_rows + jnp.arange(prompt_rows, dtype=jnp.int32)
    )
    queries_abs = absorb(prompt_queries.reshape(prompt_count * prompt_rows, -1), key_up).reshape(
        head_count, prompt_count, prompt_rows, RANK
    )
    start_state = fresh_state((head_count, prompt_count, prompt_rows))
    owners = page_owner[0]
    slot_ids = jnp.arange(PAGES_DEV, dtype=jnp.int32)
    shard_rows = lax.all_gather(latent, "cp", axis=1, tiled=True)
    running = start_state
    running = context_step(running, shard_rows, query_pos, queries_abs, block_order)
    running, whole_store = (running, shard_rows)
    slot_cap = max(1, PAGES_DEV // cycle_size)
    my_owners = lax.dynamic_index_in_dim(owners, cycle_index, 0, keepdims=False)
    same_owner = (my_owners[:, None] == my_owners[None, :]) & (
        slot_ids[None, :] < slot_ids[:, None]
    )
    send_slot = my_owners * slot_cap + jnp.sum(same_owner.astype(jnp.int32), axis=1)
    select = (
        send_slot[None, :] == jnp.arange(cycle_size * slot_cap, dtype=jnp.int32)[:, None]
    ).astype(jnp.bfloat16)
    page_rows = latent.reshape(PAGES_DEV, PAGE * 2 * RANK)
    outgoing = jnp.dot(select, page_rows, preferred_element_type=jnp.float32).astype(jnp.bfloat16)
    outgoing = outgoing.reshape(cycle_size, slot_cap * PAGE, 2 * RANK)
    incoming = lax.all_to_all(outgoing, "cp", split_axis=0, concat_axis=0, tiled=True)
    counts = jnp.sum((owners == cycle_index).astype(jnp.int32), axis=1)
    source_ids = jnp.arange(counts.shape[0], dtype=jnp.int32)
    offsets = jnp.sum(
        jnp.where(source_ids[None, :] < source_ids[:, None], counts[None, :], 0), axis=1
    )
    places = jnp.arange(slot_cap, dtype=jnp.int32)
    slot_valid = places[None, :] < counts[:, None]
    target = jnp.where(slot_valid, offsets[:, None] + places[None, :], -1).reshape(-1)
    compact = (target[None, :] == slot_ids[:, None]).astype(jnp.bfloat16)
    page_store = jnp.dot(
        compact,
        incoming.reshape(cycle_size * slot_cap, PAGE * 2 * RANK),
        preferred_element_type=jnp.float32,
    )
    page_store = page_store.astype(jnp.bfloat16).reshape(PAGES_DEV * PAGE, 2 * RANK)
    final_peak, final_total, final_sum = running
    prefill_latent = (
        (final_sum / final_total[..., None])
        .astype(jnp.bfloat16)
        .reshape(head_count, prompt_count * prompt_rows, RANK)
    )
    prefill_rows = rebuild(prefill_latent, value_up).reshape(
        prompt_count, prompt_rows, head_count * HEAD
    )
    live_rows = query_pos[None, :] < prompt_lengths[:, None]
    prefill_out = jnp.where(live_rows[..., None], prefill_rows, jnp.zeros_like(prefill_rows))
    rows_all = STEPS * ROW_GRP
    score_scale = HEAD ** (-0.5)
    decode_abs = absorb(decode_queries.reshape(rows_all, -1), key_up)
    row_prompt = jnp.arange(ROW_GRP, dtype=jnp.int32) // (ROW_GRP // PPG)
    row_limit = jnp.minimum(decode_context, lookup(prompt_lengths, row_prompt))
    step_abs = decode_abs.reshape(head_count, STEPS, ROW_GRP, RANK)
    own_scores = (
        jnp.einsum(
            "htnr,snr->htns", step_abs, new_latent[..., :RANK], preferred_element_type=jnp.float32
        )
        * score_scale
    )
    step_ids = jnp.arange(STEPS, dtype=jnp.int32)
    own_mask = (step_ids[None, :] <= step_ids[:, None])[:, None, :]
    own_values = new_latent[..., RANK:]

    def weigh_own(weights):
        return jnp.einsum("htns,snr->htnr", weights, own_values, preferred_element_type=jnp.float32)

    own_part = online(fresh_state((head_count, STEPS, ROW_GRP)), own_scores, own_mask, weigh_own)
    own_part = (
        own_part[0].reshape(head_count, rows_all),
        own_part[1].reshape(head_count, rows_all),
        own_part[2].reshape(head_count, rows_all, RANK),
    )
    share_rows = rows_all // cycle_size
    share_start = cycle_index * share_rows
    share_abs = lax.dynamic_slice_in_dim(decode_abs, share_start, share_rows, 1)
    share_ids = (share_start + jnp.arange(share_rows, dtype=jnp.int32)) % ROW_GRP
    share_prompt = lookup(row_prompt, share_ids)
    share_limit = lookup(row_limit, share_ids)
    whole_rows = whole_store.shape[1]
    whole_pos = row_positions(block_order, jnp.arange(whole_rows, dtype=jnp.int32))
    key_prompt = jnp.broadcast_to(
        jnp.arange(prompt_count, dtype=jnp.int32)[:, None], (prompt_count, whole_rows)
    ).reshape(-1)
    key_pos = jnp.broadcast_to(whole_pos[None, :], (prompt_count, whole_rows)).reshape(-1)
    flat_whole = whole_store.reshape(prompt_count * whole_rows, 2 * RANK)
    whole_mask = (key_prompt[None, :] == share_prompt[:, None]) & (
        key_pos[None, :] < share_limit[:, None]
    )
    whole_scores = (
        jnp.einsum(
            "hqr,mr->hqm", share_abs, flat_whole[:, :RANK], preferred_element_type=jnp.float32
        )
        * score_scale
    )
    whole_values = flat_whole[:, RANK:]

    def weigh_whole(weights):
        return jnp.einsum("hqm,mr->hqr", weights, whole_values, preferred_element_type=jnp.float32)

    whole_part = online(
        fresh_state((head_count, share_rows)), whole_scores, whole_mask, weigh_whole
    )
    own_share = tuple(
        (lax.dynamic_slice_in_dim(member, share_start, share_rows, 1) for member in own_part)
    )
    final_peak, final_total, final_sum = combine_parts(whole_part, own_share)
    decoded = rebuild((final_sum / final_total[..., None]).astype(jnp.bfloat16), value_up)
    decoded = lax.all_gather(decoded, "cp", axis=0, tiled=True)
    decode_out = decoded.reshape(STEPS, ROW_GRP, head_count * HEAD)
    page_cache = page_store.reshape(1, 1, PAGES_DEV * PAGE, 2 * RANK)
    return (prefill_out, decode_out, page_cache)


MESH = pl.DeviceIdType.MESH
SCHEDULES = {(4, 2): [('attend', [0], 0), ('receive', 1, 0), ('attend', [0], 1), ('receive', 1, 1), ('own', 0, 0), ('own', 0, 1), ('attend', [1], 0), ('receive', 3, 0), ('attend', [1], 1), ('receive', 3, 1), ('attend', [2], 0), ('pick', 0, 0), ('receive', 2, 0), ('attend', [2], 1), ('receive', 2, 1), ('attend', [3], 0), ('finish', 0, 0), ('attend', [3], 1), ('finish', 0, 1)]}
KEY_LIMIT = 1024


def fused_kernel(
    n,
    k_chunks,
    lengths_hbm,
    order_hbm,
    context_hbm,
    owner_hbm,
    states_hbm,
    fresh_hbm,
    down_hbm,
    queries_hbm,
    asks_hbm,
    key_up_hbm,
    value_up_hbm,
    store_ref,
    prefill_ref,
    decode_ref,
    pick_ref,
    lengths_ref,
    order_ref,
    context_ref,
    owner_ref,
    states_buf,
    fresh_buf,
    down_buf,
    queries_ref,
    asks_ref,
    key_up_ref,
    value_up_ref,
    new_ref,
    absorbed_ref,
    asked_ref,
    peak_ref,
    total_ref,
    sum_ref,
    pick_buf,
    pick_sem,
    load_sem,
    small_sem,
    send_sem,
    recv_sem,
    new_send,
    new_recv,
):
    z = lax.axis_index("cp")
    c = lax.axis_index("sec")
    other = 1 - c
    prompts, rows, width = states_hbm.shape
    heads = key_up_ref.shape[1] // HEAD
    steps, row_grp, _ = asks_ref.shape
    share = row_grp // prompts
    blocks = rows // BLOCK
    asking = heads * rows
    fresh_lanes = heads * steps * share
    lanes = asking + fresh_lanes
    factor = HEAD**-0.5 * math.log2(math.e)
    nt = (((1,), (1,)), ((), ()))
    tn = (((0,), (0,)), ((), ()))
    kw = width // k_chunks
    later_chunks = 2

    small = [
        pltpu.make_async_copy(source, held, small_sem.at[i])
        for i, (source, held) in enumerate(
            [
                (order_hbm, order_ref),
                (lengths_hbm, lengths_ref),
                (context_hbm, context_ref),
                (key_up_hbm, key_up_ref),
                (queries_hbm, queries_ref),
                (asks_hbm, asks_ref),
                (value_up_hbm, value_up_ref),
                (owner_hbm, owner_ref),
            ]
        )
    ]
    pick_copy = pltpu.make_async_copy(pick_buf, pick_ref, pick_sem)
    loads = {}
    for copy in small[:3]:
        copy.start()
    for k in range(k_chunks):
        cols = pl.ds(k * kw, kw)
        loads["w", k] = pltpu.make_async_copy(
            down_hbm.at[cols, :], down_buf.at[cols, :], load_sem.at[0, k]
        )
        loads["w", k].start()
        loads[0, k] = pltpu.make_async_copy(
            states_hbm.at[0, :, cols], states_buf.at[0, :, cols], load_sem.at[1, k]
        )
        loads[0, k].start()
    for p in range(1, prompts):
        for k in range(later_chunks):
            cols = pl.ds(k * (width // later_chunks), width // later_chunks)
            loads[p, k] = pltpu.make_async_copy(
                states_hbm.at[p, :, cols], states_buf.at[p, :, cols], load_sem.at[1 + p, k]
            )
            loads[p, k].start()
    loads["d", 0] = pltpu.make_async_copy(fresh_hbm, fresh_buf, load_sem.at[1 + prompts, 0])
    loads["d", 0].start()
    for copy in small[3:]:
        copy.start()

    barrier = pltpu.get_barrier_semaphore()
    pl.semaphore_signal(barrier, inc=1, device_id={"sec": other}, device_id_type=MESH)
    peers = jnp.int32(1)
    for gap in [g for g in range(1, n) if g != 2]:

        @pl.when(z - gap >= 0)
        def _():
            pl.semaphore_signal(barrier, inc=1, device_id={"cp": z - gap}, device_id_type=MESH)

        @pl.when(z + gap < n)
        def _():
            pl.semaphore_signal(barrier, inc=1, device_id={"cp": z + gap}, device_id_type=MESH)

        peers = peers + (z >= gap).astype(jnp.int32) + (z + gap < n).astype(jnp.int32)

    def shard_rows(shard, p):
        return pl.ds(pl.multiple_of((shard * prompts + p) * rows, rows), rows)

    def transfer(half, shard, p, way, index, target):
        piece = store_ref.at[half, shard_rows(shard, p), :]
        return pltpu.make_async_remote_copy(
            src_ref=piece,
            dst_ref=piece,
            send_sem=send_sem.at[way, index, p],
            recv_sem=recv_sem.at[half, shard, p],
            device_id=target,
            device_id_type=MESH,
        )

    def rightward(shard, p):
        return transfer(c, shard, p, 0, shard, {"cp": z + 1})

    def leftward(shard, p):
        return transfer(c, shard, p, 1, shard, {"cp": z - 1})

    def across(shard, p):
        return transfer(c, shard, p, 2, shard, {"sec": other})

    def direct(target, p):
        return transfer(c, z, p, 3, target, {"cp": target})

    def arrival(shard, p):
        return transfer(c, shard, p, 0, shard, {"cp": z})

    def wait_other(shard, p):
        transfer(other, shard, p, 2, shard, {"sec": other}).wait_recv()

    def project(kind, buf):
        chunks = {0: k_chunks, "d": 1}.get(kind, later_chunks)
        step = width // chunks
        total = jnp.zeros((buf.shape[0], down_buf.shape[1]), jnp.float32)
        for k in range(chunks):
            if kind == 0:
                loads["w", k].wait()
            loads[kind, k].wait()
            cols = pl.ds(k * step, step)
            total += jnp.dot(
                buf[:, cols], down_buf[cols, :], preferred_element_type=jnp.float32
            )
        return total.astype(jnp.bfloat16)

    def stacked(parts):
        return jnp.concatenate(parts, axis=0)

    def head_cols(h):
        return pl.ds(h * HEAD, HEAD)

    def absorb_head(rows_in, h):
        return lax.dot_general(
            rows_in, key_up_ref[:, head_cols(h)], nt, preferred_element_type=jnp.float32
        ).astype(jnp.bfloat16)

    def rebuild_head(rows_in, h):
        return jnp.dot(
            rows_in, value_up_ref[:, head_cols(h)], preferred_element_type=jnp.float32
        ).astype(jnp.bfloat16)

    def place(shard, column):
        row = lax.broadcasted_iota(jnp.int32, (rows, 1) if column else (1, asking), 1 - column)
        row = row if column else row % rows
        found = jnp.zeros_like(row)
        for b in range(blocks):
            shift = (order_ref[shard * blocks + b] - b) * BLOCK
            found = jnp.where(row // BLOCK == b, row + shift, found)
        return found

    for copy in small[:3]:
        copy.wait()
    asked_rows = place(z, 0)
    spot = lax.broadcasted_iota(jnp.int32, (1, fresh_lanes), 1)
    for p in range(prompts):
        asked_ref[p, :, pl.ds(0, asking)] = asked_rows
        limit = jnp.zeros((1, fresh_lanes), jnp.int32)
        for r in range(share):
            limit = jnp.where(
                spot % share == r,
                jnp.minimum(context_ref[p * share + r], lengths_ref[p]) - 1,
                limit,
            )
        asked_ref[p, :, pl.ds(asking, fresh_lanes)] = limit

    for p in range(prompts):
        store_ref[c, shard_rows(z, p), :] = project(p, states_buf.at[p])
        if p == 0:
            pl.semaphore_wait(barrier, peers)

        @pl.when(z > 0)
        def _():
            leftward(z, p).start()

        @pl.when(z < n - 1)
        def _():
            rightward(z, p).start()

        across(z, p).start()
        for gap in range(3, n):

            @pl.when(z - gap >= 0)
            def _():
                direct(z - gap, p).start()

            @pl.when(z + gap < n)
            def _():
                direct(z + gap, p).start()

    new_ref[c] = project("d", fresh_buf)
    new_copy = pltpu.make_async_remote_copy(
        src_ref=new_ref.at[c],
        dst_ref=new_ref.at[c],
        send_sem=new_send,
        recv_sem=new_recv,
        device_id={"sec": other},
        device_id_type=MESH,
    )
    new_copy.start()

    for copy in small[3:]:
        copy.wait()
    for p in range(prompts):
        for h in range(heads):
            absorbed_ref[p, pl.ds(h * rows, rows), :] = absorb_head(
                queries_ref[p, :, head_cols(h)], h
            )
            asks = stacked([asks_ref[t, pl.ds(p * share, share), head_cols(h)] for t in range(steps)])
            absorbed_ref[p, pl.ds(asking + h * steps * share, steps * share), :] = absorb_head(asks, h)

    fresh_at = pl.ds(asking, fresh_lanes)
    step_of = spot // share % steps

    def attend_own(p):
        mine = [pl.ds(t * row_grp + p * share, share) for t in range(steps)]
        wide = absorbed_ref[p, fresh_at, :].astype(jnp.float32).T
        own_scores = []
        for t in range(steps):
            own_key = stacked([new_ref[0, mine[t], :].astype(jnp.float32)] * (heads * steps)).T
            own = jnp.sum(wide * own_key, axis=0, keepdims=True)
            own_scores.append(jnp.where(step_of >= t, own, NEG))
        old_peak = peak_ref[p, :, fresh_at]
        peak = functools.reduce(jnp.maximum, own_scores, old_peak)
        rescale = jnp.exp2((old_peak - peak) * factor)
        total = total_ref[p, :, fresh_at] * rescale
        summed = sum_ref[p, :, fresh_at] * rescale
        for t in range(steps):
            own_weight = jnp.exp2((own_scores[t] - peak) * factor)
            total = total + own_weight
            own_value = stacked([new_ref[1, mine[t], :].astype(jnp.float32)] * (heads * steps)).T
            summed = summed + own_weight.astype(jnp.bfloat16).astype(jnp.float32) * own_value
        peak_ref[p, :, fresh_at] = peak
        total_ref[p, :, fresh_at] = total
        sum_ref[p, :, fresh_at] = summed

    def attend(shards, p, first=False):
        for shard in shards:
            wait_other(shard, p)
        key_rows = stacked([store_ref[0, shard_rows(shard, p), :] for shard in shards])
        value_rows = stacked([store_ref[1, shard_rows(shard, p), :] for shard in shards])
        key_pos = stacked([place(shard, 1) for shard in shards])
        scores = lax.dot_general(
            key_rows, absorbed_ref[p], nt, preferred_element_type=jnp.float32
        )
        scores = jnp.where(key_pos <= asked_ref[p], scores, NEG)
        peak = jnp.max(scores, axis=0, keepdims=True)
        if not first:
            old_peak = peak_ref[p]
            peak = jnp.maximum(old_peak, peak)
            rescale = jnp.exp2((old_peak - peak) * factor)
        weights = jnp.exp2((scores - peak) * factor)
        total = jnp.sum(weights, axis=0, keepdims=True)
        summed = lax.dot_general(
            value_rows, weights.astype(jnp.bfloat16), tn, preferred_element_type=jnp.float32
        )
        if not first:
            total = total_ref[p] * rescale + total
            summed = sum_ref[p] * rescale + summed
        peak_ref[p] = peak
        total_ref[p] = total
        sum_ref[p] = summed

    def finish(p):
        latent_out = (sum_ref[p] * (1.0 / total_ref[p])).T.astype(jnp.bfloat16)
        live = place(z, 1) < lengths_ref[p]
        for h in range(heads):
            rebuilt = rebuild_head(latent_out[h * rows : (h + 1) * rows], h)
            prefill_ref[p, :, head_cols(h)] = jnp.where(live, rebuilt, jnp.zeros_like(rebuilt))
            first = asking + h * steps * share
            rebuilt = rebuild_head(latent_out[first : first + steps * share], h)
            for t in range(steps):
                decode_ref[t, pl.ds(p * share, share), head_cols(h)] = rebuilt[
                    t * share : (t + 1) * share
                ]

    def pick_slots():
        slot = lax.broadcasted_iota(jnp.int32, (1, pick_buf.shape[1]), 1)
        picked = jnp.zeros_like(slot)
        count = jnp.int32(0)
        for s in range(n):
            for k in range(owner_ref.shape[2]):
                mine = owner_ref[0, s, k] == z
                picked = jnp.where(slot == jnp.where(mine, count, -1), s * owner_ref.shape[2] + k, picked)
                count = count + mine.astype(jnp.int32)
        pick_buf[...] = picked
        pick_copy.start()

    def receive(gap, p):
        @pl.when(z - gap >= 0)
        def _():
            arrival(z - gap, p).wait_recv()
            if gap == 1:

                @pl.when(z < n - 1)
                def _():
                    rightward(z - gap, p).start()

            across(z - gap, p).start()

        @pl.when(z + gap < n)
        def _():
            arrival(z + gap, p).wait_recv()
            if gap == 1:

                @pl.when(z > 0)
                def _():
                    leftward(z + gap, p).start()

            across(z + gap, p).start()

    gaps = [g for g in range(1, n) if g != 2] + [g for g in range(2, min(n, 3))]

    def source(step):
        found, passed = jnp.int32(0), jnp.int32(0)
        for gap in gaps:
            for shard, there in ((z - gap, z >= gap), (z + gap, z + gap < n)):
                passed = passed + there.astype(jnp.int32)
                found = jnp.where(there & (passed == step), shard, found)
        return found

    plan = SCHEDULES.get((n, prompts)) or (
        [("receive", gap, p) for gap in range(1, n) for p in range(prompts)]
        + [("attend", [step], p) for step in range(n) for p in range(prompts)]
        + [("own", 0, p) for p in range(prompts)]
        + [("pick", 0, 0)]
        + [("finish", 0, p) for p in range(prompts)]
    )
    begun = set()
    waited = False
    for kind, which, p in plan:
        if kind == "receive":
            receive(which, p)
        elif kind == "attend":
            attend([source(step) if step else z for step in which], p, first=p not in begun)
            begun.add(p)
        elif kind == "own":
            if not waited:
                new_copy.wait_recv()
                waited = True
            attend_own(p)
        elif kind == "finish":
            finish(p)
        else:
            pick_slots()

    for shard in range(n):
        for p in range(prompts):
            across(shard, p).wait_send()

            @pl.when((shard <= z) & (shard >= z - 1) & (z < n - 1))
            def _():
                rightward(shard, p).wait_send()

            @pl.when((shard >= z) & (shard <= z + 1) & (z > 0))
            def _():
                leftward(shard, p).wait_send()

            @pl.when((shard >= z + 3) | (shard <= z - 3))
            def _():
                direct(shard, p).wait_send()

    new_copy.wait_send()
    pick_copy.wait()


def hand_over_kernel(
    pick_ref,
    store_ref,
    prefill_ref,
    decode_ref,
    prefill_out,
    decode_out,
    page_out,
    pages_ref,
    sems,
):
    whole = [
        pltpu.make_async_copy(prefill_ref, prefill_out, sems.at[0]),
        pltpu.make_async_copy(decode_ref, decode_out, sems.at[1]),
        pltpu.make_async_copy(pages_ref, page_out, sems.at[2]),
    ]
    for copy in whole[:2]:
        copy.start()
    for slot in range(pages_ref.shape[2] // PAGE):
        page = pl.ds(pl.multiple_of(pick_ref[0, slot] * PAGE, PAGE), PAGE)
        pages_ref[0, 0, pl.ds(slot * PAGE, PAGE), :RANK] = store_ref[0, page, :]
        pages_ref[0, 0, pl.ds(slot * PAGE, PAGE), RANK:] = store_ref[1, page, :]
    whole[2].start()
    for copy in whole:
        copy.wait()


def local_small(
    n,
    prompt_states,
    prompt_queries,
    decode_states,
    decode_queries,
    latent_down,
    key_up,
    value_up,
    prompt_lengths,
    block_order,
    page_owner,
    decode_context,
):
    steps, row_grp, width = decode_states.shape
    prompts, rows, _ = prompt_states.shape
    fresh_rows = steps * row_grp
    heads = key_up.shape[1] // HEAD
    lanes = heads * (rows + steps * (row_grp // prompts))
    k_chunks = 4
    hbm = pl.BlockSpec(memory_space=pltpu.HBM)
    smem = pl.BlockSpec(memory_space=pltpu.SMEM)
    vmem = pl.BlockSpec(memory_space=pltpu.VMEM)
    operands = [
        pltpu.with_memory_space_constraint(array, pltpu.HBM)
        for array in (
            prompt_lengths,
            block_order,
            decode_context,
            page_owner,
            prompt_states,
            decode_states.reshape(fresh_rows, width),
            latent_down,
            prompt_queries,
            decode_queries,
            key_up,
            value_up,
        )
    ]
    dma = pltpu.SemaphoreType.DMA
    slots = pl.cdiv(page_owner.shape[2], 128) * 128
    store, prefill, decoded, picks = pl.pallas_call(
        functools.partial(fused_kernel, n, k_chunks),
        out_shape=(
            pltpu.VMEM((2, n * prompts * rows, RANK), jnp.bfloat16),
            pltpu.VMEM(prompt_queries.shape, jnp.bfloat16),
            pltpu.VMEM(decode_queries.shape, jnp.bfloat16),
            pltpu.SMEM((1, slots), jnp.int32),
        ),
        in_specs=[hbm] * len(operands),
        out_specs=(vmem,) * 3 + (smem,),
        scratch_shapes=[
            pltpu.SMEM(prompt_lengths.shape, jnp.int32),
            pltpu.SMEM(block_order.shape, jnp.int32),
            pltpu.SMEM(decode_context.shape, jnp.int32),
            pltpu.SMEM(page_owner.shape, jnp.int32),
            pltpu.VMEM((prompts, rows, width), jnp.bfloat16),
            pltpu.VMEM((fresh_rows, width), jnp.bfloat16),
            pltpu.VMEM(latent_down.shape, jnp.bfloat16),
            pltpu.VMEM(prompt_queries.shape, jnp.bfloat16),
            pltpu.VMEM(decode_queries.shape, jnp.bfloat16),
            pltpu.VMEM(key_up.shape, jnp.bfloat16),
            pltpu.VMEM(value_up.shape, jnp.bfloat16),
            pltpu.VMEM((2, fresh_rows, RANK), jnp.bfloat16),
            pltpu.VMEM((prompts, lanes, RANK), jnp.bfloat16),
            pltpu.VMEM((prompts, 1, lanes), jnp.int32),
            pltpu.VMEM((prompts, 1, lanes), jnp.float32),
            pltpu.VMEM((prompts, 1, lanes), jnp.float32),
            pltpu.VMEM((prompts, RANK, lanes), jnp.float32),
            pltpu.VMEM((1, slots), jnp.int32),
            dma,
            dma((2 + prompts, k_chunks)),
            dma((8,)),
            dma((4, n, prompts)),
            dma((2, n, prompts)),
            dma,
            dma,
        ],
        compiler_params=pltpu.CompilerParams(
            collective_id=0, has_side_effects=True, vmem_limit_bytes=40 * 1024 * 1024
        ),
        name="gather_attend",
    )(*operands)
    pages_dev = page_owner.shape[2]
    page_shape = (1, 1, pages_dev * PAGE, 2 * RANK)
    return pl.pallas_call(
        hand_over_kernel,
        out_shape=(
            jax.ShapeDtypeStruct(prompt_queries.shape, jnp.bfloat16),
            jax.ShapeDtypeStruct(decode_queries.shape, jnp.bfloat16),
            jax.ShapeDtypeStruct(page_shape, jnp.bfloat16),
        ),
        in_specs=[smem] + [vmem] * 3,
        out_specs=(hbm,) * 3,
        scratch_shapes=[
            pltpu.VMEM(page_shape, jnp.bfloat16),
            dma((3,)),
        ],
        compiler_params=pltpu.CompilerParams(vmem_limit_bytes=8 * 1024 * 1024),
        name="hand_over",
    )(picks, store, prefill, decoded)


def solution(mesh):
    placed = (
        P("grp", "cp", None),
        P("grp", "cp", "sec"),
        P(None, "grp", None),
        P(None, "grp", "sec"),
        P(None, "sec"),
        P(None, "sec"),
        P(None, "sec"),
        P("grp"),
        P(),
        P("grp", None, None),
        P("grp"),
    )
    n = mesh.shape["cp"]

    def on_device(prompt_states, *others):
        if n * prompt_states.shape[1] <= KEY_LIMIT and mesh.shape["sec"] == 2:
            return local_small(n, prompt_states, *others)
        return local(prompt_states, *others)

    return jax.shard_map(
        on_device,
        mesh=mesh,
        in_specs=placed,
        out_specs=(P("grp", "cp", "sec"), P(None, "grp", "sec"), P("grp", "cp", None, None)),
        check_vma=False,
    )
```

```python
import functools
import math

import jax
import jax.numpy as jnp
from jax import lax
from jax.experimental import pallas as pl
from jax.experimental.pallas import tpu as pltpu
from jax.sharding import PartitionSpec as P

HEAD = 128
RANK = 128
BLOCK = 96
PAGE = 16
PPG = 2
ROW_GRP = 32
STEPS = 3
PAGES_DEV = 24


NEG = -1e30


def lookup(table_rows, indices):
    matches = indices[..., None] == jnp.arange(table_rows.shape[0], dtype=jnp.int32)
    return jnp.sum(jnp.where(matches, table_rows, 0), axis=-1)


def row_positions(block_order, stored_rows):
    return lookup(block_order, stored_rows // BLOCK) * BLOCK + stored_rows % BLOCK


def absorb(queries, key_up):
    row_count = queries.shape[0]
    head_count = key_up.shape[1] // HEAD
    q_parts = queries.reshape(row_count, head_count, HEAD)
    u_parts = key_up.reshape(RANK, head_count, HEAD)
    return jnp.einsum("nhd,rhd->hnr", q_parts, u_parts, preferred_element_type=jnp.float32).astype(
        jnp.bfloat16
    )


def rebuild(latent_out, value_up):
    head_count = value_up.shape[1] // HEAD
    u_parts = value_up.reshape(RANK, head_count, HEAD)
    rebuilt = jnp.einsum("hnr,rhd->nhd", latent_out, u_parts, preferred_element_type=jnp.float32)
    return rebuilt.astype(jnp.bfloat16).reshape(latent_out.shape[1], head_count * HEAD)


def fresh_state(row_shape):
    return (
        jnp.full(row_shape, NEG, jnp.float32),
        jnp.zeros(row_shape, jnp.float32),
        jnp.zeros(row_shape + (RANK,), jnp.float32),
    )


def online(running, scores, key_mask, weigh_fn):
    old_peak, old_total, old_sum = running
    scores = jnp.where(key_mask, scores, NEG)
    new_peak = jnp.maximum(old_peak, jnp.max(scores, axis=-1))
    factor = jnp.exp(old_peak - new_peak)
    weights = jnp.where(key_mask, jnp.exp(scores - new_peak[..., None]), 0.0)
    new_total = old_total * factor + jnp.sum(weights, axis=-1)
    new_sum = old_sum * factor[..., None] + weigh_fn(weights.astype(jnp.bfloat16))
    return (new_peak, new_total, new_sum)


def combine_parts(earlier, second):
    joined_peak = jnp.maximum(earlier[0], second[0])
    left_scale = jnp.exp(earlier[0] - joined_peak)
    right_scale = jnp.exp(second[0] - joined_peak)
    joined_total = earlier[1] * left_scale + second[1] * right_scale
    joined_sum = earlier[2] * left_scale[..., None] + second[2] * right_scale[..., None]
    return (joined_peak, joined_total, joined_sum)


def context_step(running, shard_rows, query_pos, queries_abs, block_order):
    row_count = shard_rows.shape[1]
    key_pos = row_positions(block_order, jnp.arange(row_count, dtype=jnp.int32))
    score_scale = HEAD ** (-0.5)
    for block_start in range(0, row_count, 1024):
        block_end = min(row_count, block_start + 1024)
        key_block = shard_rows[:, block_start:block_end, :RANK]
        value_block = shard_rows[:, block_start:block_end, RANK:]
        key_mask = key_pos[block_start:block_end][None, :] <= query_pos[:, None]
        scores = (
            jnp.einsum("hpnr,pmr->hpnm", queries_abs, key_block, preferred_element_type=jnp.float32)
            * score_scale
        )

        def weigh_block(weights, value_block=value_block):
            return jnp.einsum(
                "hpnm,pmr->hpnr", weights, value_block, preferred_element_type=jnp.float32
            )

        running = online(running, scores, key_mask, weigh_block)
    return running


def local(
    prompt_states,
    prompt_queries,
    decode_states,
    decode_queries,
    latent_down,
    key_up,
    value_up,
    prompt_lengths,
    block_order,
    page_owner,
    decode_context,
):
    prompt_count, prompt_rows, model_width = prompt_states.shape
    cycle_index = lax.axis_index("cp")
    cycle_size = lax.axis_size("cp")
    head_count = key_up.shape[1] // HEAD
    lat_half = jnp.dot(
        prompt_states.reshape(prompt_count * prompt_rows, model_width),
        latent_down,
        preferred_element_type=jnp.float32,
    )
    lat_half = lat_half.astype(jnp.bfloat16).reshape(prompt_count, prompt_rows, RANK)
    new_half = jnp.dot(
        decode_states.reshape(STEPS * ROW_GRP, model_width),
        latent_down,
        preferred_element_type=jnp.float32,
    )
    new_half = new_half.astype(jnp.bfloat16).reshape(STEPS, ROW_GRP, RANK)
    latent, new_latent = (
        lax.all_gather(lat_half, "sec", axis=2, tiled=True),
        lax.all_gather(new_half, "sec", axis=2, tiled=True),
    )
    query_pos = row_positions(
        block_order, cycle_index * prompt_rows + jnp.arange(prompt_rows, dtype=jnp.int32)
    )
    queries_abs = absorb(prompt_queries.reshape(prompt_count * prompt_rows, -1), key_up).reshape(
        head_count, prompt_count, prompt_rows, RANK
    )
    start_state = fresh_state((head_count, prompt_count, prompt_rows))
    owners = page_owner[0]
    slot_ids = jnp.arange(PAGES_DEV, dtype=jnp.int32)
    shard_rows = lax.all_gather(latent, "cp", axis=1, tiled=True)
    running = start_state
    running = context_step(running, shard_rows, query_pos, queries_abs, block_order)
    running, whole_store = (running, shard_rows)
    slot_cap = max(1, PAGES_DEV // cycle_size)
    my_owners = lax.dynamic_index_in_dim(owners, cycle_index, 0, keepdims=False)
    same_owner = (my_owners[:, None] == my_owners[None, :]) & (
        slot_ids[None, :] < slot_ids[:, None]
    )
    send_slot = my_owners * slot_cap + jnp.sum(same_owner.astype(jnp.int32), axis=1)
    select = (
        send_slot[None, :] == jnp.arange(cycle_size * slot_cap, dtype=jnp.int32)[:, None]
    ).astype(jnp.bfloat16)
    page_rows = latent.reshape(PAGES_DEV, PAGE * 2 * RANK)
    outgoing = jnp.dot(select, page_rows, preferred_element_type=jnp.float32).astype(jnp.bfloat16)
    outgoing = outgoing.reshape(cycle_size, slot_cap * PAGE, 2 * RANK)
    incoming = lax.all_to_all(outgoing, "cp", split_axis=0, concat_axis=0, tiled=True)
    counts = jnp.sum((owners == cycle_index).astype(jnp.int32), axis=1)
    source_ids = jnp.arange(counts.shape[0], dtype=jnp.int32)
    offsets = jnp.sum(
        jnp.where(source_ids[None, :] < source_ids[:, None], counts[None, :], 0), axis=1
    )
    places = jnp.arange(slot_cap, dtype=jnp.int32)
    slot_valid = places[None, :] < counts[:, None]
    target = jnp.where(slot_valid, offsets[:, None] + places[None, :], -1).reshape(-1)
    compact = (target[None, :] == slot_ids[:, None]).astype(jnp.bfloat16)
    page_store = jnp.dot(
        compact,
        incoming.reshape(cycle_size * slot_cap, PAGE * 2 * RANK),
        preferred_element_type=jnp.float32,
    )
    page_store = page_store.astype(jnp.bfloat16).reshape(PAGES_DEV * PAGE, 2 * RANK)
    final_peak, final_total, final_sum = running
    prefill_latent = (
        (final_sum / final_total[..., None])
        .astype(jnp.bfloat16)
        .reshape(head_count, prompt_count * prompt_rows, RANK)
    )
    prefill_rows = rebuild(prefill_latent, value_up).reshape(
        prompt_count, prompt_rows, head_count * HEAD
    )
    live_rows = query_pos[None, :] < prompt_lengths[:, None]
    prefill_out = jnp.where(live_rows[..., None], prefill_rows, jnp.zeros_like(prefill_rows))
    rows_all = STEPS * ROW_GRP
    score_scale = HEAD ** (-0.5)
    decode_abs = absorb(decode_queries.reshape(rows_all, -1), key_up)
    row_prompt = jnp.arange(ROW_GRP, dtype=jnp.int32) // (ROW_GRP // PPG)
    row_limit = jnp.minimum(decode_context, lookup(prompt_lengths, row_prompt))
    step_abs = decode_abs.reshape(head_count, STEPS, ROW_GRP, RANK)
    own_scores = (
        jnp.einsum(
            "htnr,snr->htns", step_abs, new_latent[..., :RANK], preferred_element_type=jnp.float32
        )
        * score_scale
    )
    step_ids = jnp.arange(STEPS, dtype=jnp.int32)
    own_mask = (step_ids[None, :] <= step_ids[:, None])[:, None, :]
    own_values = new_latent[..., RANK:]

    def weigh_own(weights):
        return jnp.einsum("htns,snr->htnr", weights, own_values, preferred_element_type=jnp.float32)

    own_part = online(fresh_state((head_count, STEPS, ROW_GRP)), own_scores, own_mask, weigh_own)
    own_part = (
        own_part[0].reshape(head_count, rows_all),
        own_part[1].reshape(head_count, rows_all),
        own_part[2].reshape(head_count, rows_all, RANK),
    )
    share_rows = rows_all // cycle_size
    share_start = cycle_index * share_rows
    share_abs = lax.dynamic_slice_in_dim(decode_abs, share_start, share_rows, 1)
    share_ids = (share_start + jnp.arange(share_rows, dtype=jnp.int32)) % ROW_GRP
    share_prompt = lookup(row_prompt, share_ids)
    share_limit = lookup(row_limit, share_ids)
    whole_rows = whole_store.shape[1]
    whole_pos = row_positions(block_order, jnp.arange(whole_rows, dtype=jnp.int32))
    key_prompt = jnp.broadcast_to(
        jnp.arange(prompt_count, dtype=jnp.int32)[:, None], (prompt_count, whole_rows)
    ).reshape(-1)
    key_pos = jnp.broadcast_to(whole_pos[None, :], (prompt_count, whole_rows)).reshape(-1)
    flat_whole = whole_store.reshape(prompt_count * whole_rows, 2 * RANK)
    whole_mask = (key_prompt[None, :] == share_prompt[:, None]) & (
        key_pos[None, :] < share_limit[:, None]
    )
    whole_scores = (
        jnp.einsum(
            "hqr,mr->hqm", share_abs, flat_whole[:, :RANK], preferred_element_type=jnp.float32
        )
        * score_scale
    )
    whole_values = flat_whole[:, RANK:]

    def weigh_whole(weights):
        return jnp.einsum("hqm,mr->hqr", weights, whole_values, preferred_element_type=jnp.float32)

    whole_part = online(
        fresh_state((head_count, share_rows)), whole_scores, whole_mask, weigh_whole
    )
    own_share = tuple(
        (lax.dynamic_slice_in_dim(member, share_start, share_rows, 1) for member in own_part)
    )
    final_peak, final_total, final_sum = combine_parts(whole_part, own_share)
    decoded = rebuild((final_sum / final_total[..., None]).astype(jnp.bfloat16), value_up)
    decoded = lax.all_gather(decoded, "cp", axis=0, tiled=True)
    decode_out = decoded.reshape(STEPS, ROW_GRP, head_count * HEAD)
    page_cache = page_store.reshape(1, 1, PAGES_DEV * PAGE, 2 * RANK)
    return (prefill_out, decode_out, page_cache)


MESH = pl.DeviceIdType.MESH
SCHEDULES = {(4, 2): [('attend', [0], 0), ('receive', 1, 0), ('attend', [0], 1), ('receive', 1, 1), ('own', 0, 0), ('own', 0, 1), ('attend', [1], 0), ('receive', 3, 0), ('attend', [1], 1), ('receive', 3, 1), ('attend', [2], 0), ('pick', 0, 0), ('receive', 2, 0), ('attend', [2], 1), ('receive', 2, 1), ('attend', [3], 0), ('finish', 0, 0), ('attend', [3], 1), ('finish', 0, 1)]}
KEY_LIMIT = 1024


def fused_kernel(
    n,
    k_chunks,
    lengths_hbm,
    order_hbm,
    context_hbm,
    owner_hbm,
    states_hbm,
    fresh_hbm,
    down_hbm,
    queries_hbm,
    asks_hbm,
    key_up_hbm,
    value_up_hbm,
    store_ref,
    prefill_ref,
    decode_ref,
    pick_ref,
    lengths_ref,
    order_ref,
    context_ref,
    owner_ref,
    states_buf,
    fresh_buf,
    down_buf,
    queries_ref,
    asks_ref,
    key_up_ref,
    value_up_ref,
    new_ref,
    absorbed_ref,
    asked_ref,
    peak_ref,
    total_ref,
    sum_ref,
    pick_buf,
    pick_sem,
    load_sem,
    small_sem,
    send_sem,
    recv_sem,
    new_send,
    new_recv,
):
    z = lax.axis_index("cp")
    c = lax.axis_index("sec")
    other = 1 - c
    prompts, rows, width = states_hbm.shape
    heads = key_up_ref.shape[1] // HEAD
    steps, row_grp, _ = asks_ref.shape
    share = row_grp // prompts
    blocks = rows // BLOCK
    asking = heads * rows
    fresh_lanes = heads * steps * share
    lanes = asking + fresh_lanes
    factor = HEAD**-0.5 * math.log2(math.e)
    nt = (((1,), (1,)), ((), ()))
    tn = (((0,), (0,)), ((), ()))
    kw = width // k_chunks
    later_chunks = 4

    small = [
        pltpu.make_async_copy(source, held, small_sem.at[i])
        for i, (source, held) in enumerate(
            [
                (order_hbm, order_ref),
                (lengths_hbm, lengths_ref),
                (context_hbm, context_ref),
                (key_up_hbm, key_up_ref),
                (queries_hbm, queries_ref),
                (asks_hbm, asks_ref),
                (value_up_hbm, value_up_ref),
                (owner_hbm, owner_ref),
            ]
        )
    ]
    pick_copy = pltpu.make_async_copy(pick_buf, pick_ref, pick_sem)
    loads = {}
    for copy in small[:3]:
        copy.start()
    for k in range(k_chunks):
        cols = pl.ds(k * kw, kw)
        loads["w", k] = pltpu.make_async_copy(
            down_hbm.at[cols, :], down_buf.at[cols, :], load_sem.at[0, k]
        )
        loads["w", k].start()
        loads[0, k] = pltpu.make_async_copy(
            states_hbm.at[0, :, cols], states_buf.at[0, :, cols], load_sem.at[1, k]
        )
        loads[0, k].start()
    for p in range(1, prompts):
        for k in range(later_chunks):
            cols = pl.ds(k * (width // later_chunks), width // later_chunks)
            loads[p, k] = pltpu.make_async_copy(
                states_hbm.at[p, :, cols], states_buf.at[p, :, cols], load_sem.at[1 + p, k]
            )
            loads[p, k].start()
    loads["d", 0] = pltpu.make_async_copy(fresh_hbm, fresh_buf, load_sem.at[1 + prompts, 0])
    loads["d", 0].start()
    for copy in small[3:]:
        copy.start()

    barrier = pltpu.get_barrier_semaphore()
    pl.semaphore_signal(barrier, inc=1, device_id={"sec": other}, device_id_type=MESH)
    peers = jnp.int32(1)
    for gap in [g for g in range(1, n) if g != 2]:

        @pl.when(z - gap >= 0)
        def _():
            pl.semaphore_signal(barrier, inc=1, device_id={"cp": z - gap}, device_id_type=MESH)

        @pl.when(z + gap < n)
        def _():
            pl.semaphore_signal(barrier, inc=1, device_id={"cp": z + gap}, device_id_type=MESH)

        peers = peers + (z >= gap).astype(jnp.int32) + (z + gap < n).astype(jnp.int32)

    def shard_rows(shard, p):
        return pl.ds(pl.multiple_of((shard * prompts + p) * rows, rows), rows)

    def transfer(half, shard, p, way, index, target):
        piece = store_ref.at[half, shard_rows(shard, p), :]
        return pltpu.make_async_remote_copy(
            src_ref=piece,
            dst_ref=piece,
            send_sem=send_sem.at[way, index, p],
            recv_sem=recv_sem.at[half, shard, p],
            device_id=target,
            device_id_type=MESH,
        )

    def rightward(shard, p):
        return transfer(c, shard, p, 0, shard, {"cp": z + 1})

    def leftward(shard, p):
        return transfer(c, shard, p, 1, shard, {"cp": z - 1})

    def across(shard, p):
        return transfer(c, shard, p, 2, shard, {"sec": other})

    def direct(target, p):
        return transfer(c, z, p, 3, target, {"cp": target})

    def arrival(shard, p):
        return transfer(c, shard, p, 0, shard, {"cp": z})

    def wait_other(shard, p):
        transfer(other, shard, p, 2, shard, {"sec": other}).wait_recv()

    def project(kind, buf):
        chunks = {0: k_chunks, "d": 1}.get(kind, later_chunks)
        step = width // chunks
        total = jnp.zeros((buf.shape[0], down_buf.shape[1]), jnp.float32)
        for k in range(chunks):
            if kind == 0:
                loads["w", k].wait()
            loads[kind, k].wait()
            cols = pl.ds(k * step, step)
            total += jnp.dot(
                buf[:, cols], down_buf[cols, :], preferred_element_type=jnp.float32
            )
        return total.astype(jnp.bfloat16)

    def stacked(parts):
        return jnp.concatenate(parts, axis=0)

    def head_cols(h):
        return pl.ds(h * HEAD, HEAD)

    def absorb_head(rows_in, h):
        return lax.dot_general(
            rows_in, key_up_ref[:, head_cols(h)], nt, preferred_element_type=jnp.float32
        ).astype(jnp.bfloat16)

    def rebuild_head(rows_in, h):
        return jnp.dot(
            rows_in, value_up_ref[:, head_cols(h)], preferred_element_type=jnp.float32
        ).astype(jnp.bfloat16)

    def place(shard, column):
        row = lax.broadcasted_iota(jnp.int32, (rows, 1) if column else (1, asking), 1 - column)
        row = row if column else row % rows
        found = jnp.zeros_like(row)
        for b in range(blocks):
            shift = (order_ref[shard * blocks + b] - b) * BLOCK
            found = jnp.where(row // BLOCK == b, row + shift, found)
        return found

    for copy in small[:3]:
        copy.wait()
    asked_rows = place(z, 0)
    spot = lax.broadcasted_iota(jnp.int32, (1, fresh_lanes), 1)
    for p in range(prompts):
        asked_ref[p, :, pl.ds(0, asking)] = asked_rows
        limit = jnp.zeros((1, fresh_lanes), jnp.int32)
        for r in range(share):
            limit = jnp.where(
                spot % share == r,
                jnp.minimum(context_ref[p * share + r], lengths_ref[p]) - 1,
                limit,
            )
        asked_ref[p, :, pl.ds(asking, fresh_lanes)] = limit

    for p in range(prompts):
        store_ref[c, shard_rows(z, p), :] = project(p, states_buf.at[p])
        if p == 0:
            pl.semaphore_wait(barrier, peers)

        @pl.when(z > 0)
        def _():
            leftward(z, p).start()

        @pl.when(z < n - 1)
        def _():
            rightward(z, p).start()

        across(z, p).start()
        for gap in range(3, n):

            @pl.when(z - gap >= 0)
            def _():
                direct(z - gap, p).start()

            @pl.when(z + gap < n)
            def _():
                direct(z + gap, p).start()

    new_ref[c] = project("d", fresh_buf)
    new_copy = pltpu.make_async_remote_copy(
        src_ref=new_ref.at[c],
        dst_ref=new_ref.at[c],
        send_sem=new_send,
        recv_sem=new_recv,
        device_id={"sec": other},
        device_id_type=MESH,
    )
    new_copy.start()

    for copy in small[3:]:
        copy.wait()
    for p in range(prompts):
        for h in range(heads):
            absorbed_ref[p, pl.ds(h * rows, rows), :] = absorb_head(
                queries_ref[p, :, head_cols(h)], h
            )
            asks = stacked([asks_ref[t, pl.ds(p * share, share), head_cols(h)] for t in range(steps)])
            absorbed_ref[p, pl.ds(asking + h * steps * share, steps * share), :] = absorb_head(asks, h)

    fresh_at = pl.ds(asking, fresh_lanes)
    step_of = spot // share % steps

    def attend_own(p):
        mine = [pl.ds(t * row_grp + p * share, share) for t in range(steps)]
        wide = absorbed_ref[p, fresh_at, :].astype(jnp.float32).T
        own_scores = []
        for t in range(steps):
            own_key = stacked([new_ref[0, mine[t], :].astype(jnp.float32)] * (heads * steps)).T
            own = jnp.sum(wide * own_key, axis=0, keepdims=True)
            own_scores.append(jnp.where(step_of >= t, own, NEG))
        old_peak = peak_ref[p, :, fresh_at]
        peak = functools.reduce(jnp.maximum, own_scores, old_peak)
        rescale = jnp.exp2((old_peak - peak) * factor)
        total = total_ref[p, :, fresh_at] * rescale
        summed = sum_ref[p, :, fresh_at] * rescale
        for t in range(steps):
            own_weight = jnp.exp2((own_scores[t] - peak) * factor)
            total = total + own_weight
            own_value = stacked([new_ref[1, mine[t], :].astype(jnp.float32)] * (heads * steps)).T
            summed = summed + own_weight.astype(jnp.bfloat16).astype(jnp.float32) * own_value
        peak_ref[p, :, fresh_at] = peak
        total_ref[p, :, fresh_at] = total
        sum_ref[p, :, fresh_at] = summed

    def attend(shards, p, first=False):
        for shard in shards:
            wait_other(shard, p)
        key_rows = stacked([store_ref[0, shard_rows(shard, p), :] for shard in shards])
        value_rows = stacked([store_ref[1, shard_rows(shard, p), :] for shard in shards])
        scores = lax.dot_general(
            key_rows, absorbed_ref[p], nt, preferred_element_type=jnp.float32
        )
        asked = asked_ref[p]
        if first:
            key_pos = stacked([place(shard, 1) for shard in shards])
            scores = jnp.where(key_pos <= asked, scores, NEG)
            peak = jnp.max(scores, axis=0, keepdims=True)
            weights = jnp.exp2((scores - peak) * factor)
        else:
            seen = scores[:, :asking]
            starts = [order_ref[shard * blocks + b] * BLOCK for shard in shards for b in range(blocks)]
            allowed = [start <= asked[:, :asking] for start in starts]
            tiles = [seen[b * BLOCK : (b + 1) * BLOCK] for b in range(len(starts))]
            tops = [
                jnp.where(allow, jnp.max(tile, axis=0, keepdims=True), NEG)
                for allow, tile in zip(allowed, tiles)
            ]
            key_pos = stacked([place(shard, 1) for shard in shards])
            fresh = jnp.where(key_pos <= asked[:, asking:], scores[:, asking:], NEG)
            top = jnp.concatenate(
                [functools.reduce(jnp.maximum, tops), jnp.max(fresh, axis=0, keepdims=True)], axis=1
            )
            old_peak = peak_ref[p]
            peak = jnp.maximum(old_peak, top)
            rescale = jnp.exp2((old_peak - peak) * factor)
            weights = jnp.concatenate(
                [
                    stacked(
                        [
                            jnp.exp2((tile - jnp.where(allow, peak[:, :asking], -NEG)) * factor)
                            for allow, tile in zip(allowed, tiles)
                        ]
                    ),
                    jnp.exp2((fresh - peak[:, asking:]) * factor),
                ],
                axis=1,
            )
        total = jnp.sum(weights, axis=0, keepdims=True)
        summed = lax.dot_general(
            value_rows, weights.astype(jnp.bfloat16), tn, preferred_element_type=jnp.float32
        )
        if not first:
            total = total_ref[p] * rescale + total
            summed = sum_ref[p] * rescale + summed
        peak_ref[p] = peak
        total_ref[p] = total
        sum_ref[p] = summed

    def finish(p):
        latent_out = (sum_ref[p] * (1.0 / total_ref[p])).T.astype(jnp.bfloat16)
        live = place(z, 1) < lengths_ref[p]
        for h in range(heads):
            rebuilt = rebuild_head(latent_out[h * rows : (h + 1) * rows], h)
            prefill_ref[p, :, head_cols(h)] = jnp.where(live, rebuilt, jnp.zeros_like(rebuilt))
            first = asking + h * steps * share
            rebuilt = rebuild_head(latent_out[first : first + steps * share], h)
            for t in range(steps):
                decode_ref[t, pl.ds(p * share, share), head_cols(h)] = rebuilt[
                    t * share : (t + 1) * share
                ]

    def pick_slots():
        slot = lax.broadcasted_iota(jnp.int32, (1, pick_buf.shape[1]), 1)
        picked = jnp.zeros_like(slot)
        count = jnp.int32(0)
        for s in range(n):
            for k in range(owner_ref.shape[2]):
                mine = owner_ref[0, s, k] == z
                picked = jnp.where(slot == jnp.where(mine, count, -1), s * owner_ref.shape[2] + k, picked)
                count = count + mine.astype(jnp.int32)
        pick_buf[...] = picked
        pick_copy.start()

    def receive(gap, p):
        @pl.when(z - gap >= 0)
        def _():
            arrival(z - gap, p).wait_recv()
            if gap == 1:

                @pl.when(z < n - 1)
                def _():
                    rightward(z - gap, p).start()

            across(z - gap, p).start()

        @pl.when(z + gap < n)
        def _():
            arrival(z + gap, p).wait_recv()
            if gap == 1:

                @pl.when(z > 0)
                def _():
                    leftward(z + gap, p).start()

            across(z + gap, p).start()

    gaps = [g for g in range(1, n) if g != 2] + [g for g in range(2, min(n, 3))]

    def source(step):
        found, passed = jnp.int32(0), jnp.int32(0)
        for gap in gaps:
            for shard, there in ((z - gap, z >= gap), (z + gap, z + gap < n)):
                passed = passed + there.astype(jnp.int32)
                found = jnp.where(there & (passed == step), shard, found)
        return found

    plan = SCHEDULES.get((n, prompts)) or (
        [("receive", gap, p) for gap in range(1, n) for p in range(prompts)]
        + [("attend", [step], p) for step in range(n) for p in range(prompts)]
        + [("own", 0, p) for p in range(prompts)]
        + [("pick", 0, 0)]
        + [("finish", 0, p) for p in range(prompts)]
    )
    begun = set()
    waited = False
    for kind, which, p in plan:
        if kind == "receive":
            receive(which, p)
        elif kind == "attend":
            attend([source(step) if step else z for step in which], p, first=p not in begun)
            begun.add(p)
        elif kind == "own":
            if not waited:
                new_copy.wait_recv()
                waited = True
            attend_own(p)
        elif kind == "finish":
            finish(p)
        else:
            pick_slots()

    for shard in range(n):
        for p in range(prompts):
            across(shard, p).wait_send()

            @pl.when((shard <= z) & (shard >= z - 1) & (z < n - 1))
            def _():
                rightward(shard, p).wait_send()

            @pl.when((shard >= z) & (shard <= z + 1) & (z > 0))
            def _():
                leftward(shard, p).wait_send()

            @pl.when((shard >= z + 3) | (shard <= z - 3))
            def _():
                direct(shard, p).wait_send()

    new_copy.wait_send()
    pick_copy.wait()


def hand_over_kernel(
    pick_ref,
    store_ref,
    prefill_ref,
    decode_ref,
    prefill_out,
    decode_out,
    page_out,
    pages_ref,
    sems,
):
    whole = [
        pltpu.make_async_copy(prefill_ref, prefill_out, sems.at[0]),
        pltpu.make_async_copy(decode_ref, decode_out, sems.at[1]),
        pltpu.make_async_copy(pages_ref, page_out, sems.at[2]),
    ]
    for copy in whole[:2]:
        copy.start()
    for slot in range(pages_ref.shape[2] // PAGE):
        page = pl.ds(pl.multiple_of(pick_ref[0, slot] * PAGE, PAGE), PAGE)
        pages_ref[0, 0, pl.ds(slot * PAGE, PAGE), :RANK] = store_ref[0, page, :]
        pages_ref[0, 0, pl.ds(slot * PAGE, PAGE), RANK:] = store_ref[1, page, :]
    whole[2].start()
    for copy in whole:
        copy.wait()


def local_small(
    n,
    prompt_states,
    prompt_queries,
    decode_states,
    decode_queries,
    latent_down,
    key_up,
    value_up,
    prompt_lengths,
    block_order,
    page_owner,
    decode_context,
):
    steps, row_grp, width = decode_states.shape
    prompts, rows, _ = prompt_states.shape
    fresh_rows = steps * row_grp
    heads = key_up.shape[1] // HEAD
    lanes = heads * (rows + steps * (row_grp // prompts))
    k_chunks = 4
    hbm = pl.BlockSpec(memory_space=pltpu.HBM)
    smem = pl.BlockSpec(memory_space=pltpu.SMEM)
    vmem = pl.BlockSpec(memory_space=pltpu.VMEM)
    operands = [
        pltpu.with_memory_space_constraint(array, pltpu.HBM)
        for array in (
            prompt_lengths,
            block_order,
            decode_context,
            page_owner,
            prompt_states,
            decode_states.reshape(fresh_rows, width),
            latent_down,
            prompt_queries,
            decode_queries,
            key_up,
            value_up,
        )
    ]
    dma = pltpu.SemaphoreType.DMA
    slots = pl.cdiv(page_owner.shape[2], 128) * 128
    store, prefill, decoded, picks = pl.pallas_call(
        functools.partial(fused_kernel, n, k_chunks),
        out_shape=(
            pltpu.VMEM((2, n * prompts * rows, RANK), jnp.bfloat16),
            pltpu.VMEM(prompt_queries.shape, jnp.bfloat16),
            pltpu.VMEM(decode_queries.shape, jnp.bfloat16),
            pltpu.SMEM((1, slots), jnp.int32),
        ),
        in_specs=[hbm] * len(operands),
        out_specs=(vmem,) * 3 + (smem,),
        scratch_shapes=[
            pltpu.SMEM(prompt_lengths.shape, jnp.int32),
            pltpu.SMEM(block_order.shape, jnp.int32),
            pltpu.SMEM(decode_context.shape, jnp.int32),
            pltpu.SMEM(page_owner.shape, jnp.int32),
            pltpu.VMEM((prompts, rows, width), jnp.bfloat16),
            pltpu.VMEM((fresh_rows, width), jnp.bfloat16),
            pltpu.VMEM(latent_down.shape, jnp.bfloat16),
            pltpu.VMEM(prompt_queries.shape, jnp.bfloat16),
            pltpu.VMEM(decode_queries.shape, jnp.bfloat16),
            pltpu.VMEM(key_up.shape, jnp.bfloat16),
            pltpu.VMEM(value_up.shape, jnp.bfloat16),
            pltpu.VMEM((2, fresh_rows, RANK), jnp.bfloat16),
            pltpu.VMEM((prompts, lanes, RANK), jnp.bfloat16),
            pltpu.VMEM((prompts, 1, lanes), jnp.int32),
            pltpu.VMEM((prompts, 1, lanes), jnp.float32),
            pltpu.VMEM((prompts, 1, lanes), jnp.float32),
            pltpu.VMEM((prompts, RANK, lanes), jnp.float32),
            pltpu.VMEM((1, slots), jnp.int32),
            dma,
            dma((2 + prompts, k_chunks)),
            dma((8,)),
            dma((4, n, prompts)),
            dma((2, n, prompts)),
            dma,
            dma,
        ],
        compiler_params=pltpu.CompilerParams(
            collective_id=0, has_side_effects=True, vmem_limit_bytes=40 * 1024 * 1024
        ),
        name="gather_attend",
    )(*operands)
    pages_dev = page_owner.shape[2]
    page_shape = (1, 1, pages_dev * PAGE, 2 * RANK)
    return pl.pallas_call(
        hand_over_kernel,
        out_shape=(
            jax.ShapeDtypeStruct(prompt_queries.shape, jnp.bfloat16),
            jax.ShapeDtypeStruct(decode_queries.shape, jnp.bfloat16),
            jax.ShapeDtypeStruct(page_shape, jnp.bfloat16),
        ),
        in_specs=[smem] + [vmem] * 3,
        out_specs=(hbm,) * 3,
        scratch_shapes=[
            pltpu.VMEM(page_shape, jnp.bfloat16),
            dma((3,)),
        ],
        compiler_params=pltpu.CompilerParams(vmem_limit_bytes=8 * 1024 * 1024),
        name="hand_over",
    )(picks, store, prefill, decoded)


def solution(mesh):
    placed = (
        P("grp", "cp", None),
        P("grp", "cp", "sec"),
        P(None, "grp", None),
        P(None, "grp", "sec"),
        P(None, "sec"),
        P(None, "sec"),
        P(None, "sec"),
        P("grp"),
        P(),
        P("grp", None, None),
        P("grp"),
    )
    n = mesh.shape["cp"]

    def on_device(prompt_states, *others):
        if n * prompt_states.shape[1] <= KEY_LIMIT and mesh.shape["sec"] == 2:
            return local_small(n, prompt_states, *others)
        return local(prompt_states, *others)

    return jax.shard_map(
        on_device,
        mesh=mesh,
        in_specs=placed,
        out_specs=(P("grp", "cp", "sec"), P(None, "grp", "sec"), P("grp", "cp", None, None)),
        check_vma=False,
    )
```

```python
import functools
import math

import jax
import jax.numpy as jnp
from jax import lax
from jax.experimental import pallas as pl
from jax.experimental.pallas import tpu as pltpu
from jax.sharding import PartitionSpec as P

HEAD = 128
RANK = 128
BLOCK = 96
PAGE = 16
PPG = 2
ROW_GRP = 32
STEPS = 3
PAGES_DEV = 24


NEG = -1e30


def lookup(table_rows, indices):
    matches = indices[..., None] == jnp.arange(table_rows.shape[0], dtype=jnp.int32)
    return jnp.sum(jnp.where(matches, table_rows, 0), axis=-1)


def row_positions(block_order, stored_rows):
    return lookup(block_order, stored_rows // BLOCK) * BLOCK + stored_rows % BLOCK


def absorb(queries, key_up):
    row_count = queries.shape[0]
    head_count = key_up.shape[1] // HEAD
    q_parts = queries.reshape(row_count, head_count, HEAD)
    u_parts = key_up.reshape(RANK, head_count, HEAD)
    return jnp.einsum("nhd,rhd->hnr", q_parts, u_parts, preferred_element_type=jnp.float32).astype(
        jnp.bfloat16
    )


def rebuild(latent_out, value_up):
    head_count = value_up.shape[1] // HEAD
    u_parts = value_up.reshape(RANK, head_count, HEAD)
    rebuilt = jnp.einsum("hnr,rhd->nhd", latent_out, u_parts, preferred_element_type=jnp.float32)
    return rebuilt.astype(jnp.bfloat16).reshape(latent_out.shape[1], head_count * HEAD)


def fresh_state(row_shape):
    return (
        jnp.full(row_shape, NEG, jnp.float32),
        jnp.zeros(row_shape, jnp.float32),
        jnp.zeros(row_shape + (RANK,), jnp.float32),
    )


def online(running, scores, key_mask, weigh_fn):
    old_peak, old_total, old_sum = running
    scores = jnp.where(key_mask, scores, NEG)
    new_peak = jnp.maximum(old_peak, jnp.max(scores, axis=-1))
    factor = jnp.exp(old_peak - new_peak)
    weights = jnp.where(key_mask, jnp.exp(scores - new_peak[..., None]), 0.0)
    new_total = old_total * factor + jnp.sum(weights, axis=-1)
    new_sum = old_sum * factor[..., None] + weigh_fn(weights.astype(jnp.bfloat16))
    return (new_peak, new_total, new_sum)


def combine_parts(earlier, second):
    joined_peak = jnp.maximum(earlier[0], second[0])
    left_scale = jnp.exp(earlier[0] - joined_peak)
    right_scale = jnp.exp(second[0] - joined_peak)
    joined_total = earlier[1] * left_scale + second[1] * right_scale
    joined_sum = earlier[2] * left_scale[..., None] + second[2] * right_scale[..., None]
    return (joined_peak, joined_total, joined_sum)


def context_step(running, shard_rows, query_pos, queries_abs, block_order):
    row_count = shard_rows.shape[1]
    key_pos = row_positions(block_order, jnp.arange(row_count, dtype=jnp.int32))
    score_scale = HEAD ** (-0.5)
    for block_start in range(0, row_count, 1024):
        block_end = min(row_count, block_start + 1024)
        key_block = shard_rows[:, block_start:block_end, :RANK]
        value_block = shard_rows[:, block_start:block_end, RANK:]
        key_mask = key_pos[block_start:block_end][None, :] <= query_pos[:, None]
        scores = (
            jnp.einsum("hpnr,pmr->hpnm", queries_abs, key_block, preferred_element_type=jnp.float32)
            * score_scale
        )

        def weigh_block(weights, value_block=value_block):
            return jnp.einsum(
                "hpnm,pmr->hpnr", weights, value_block, preferred_element_type=jnp.float32
            )

        running = online(running, scores, key_mask, weigh_block)
    return running


def local(
    prompt_states,
    prompt_queries,
    decode_states,
    decode_queries,
    latent_down,
    key_up,
    value_up,
    prompt_lengths,
    block_order,
    page_owner,
    decode_context,
):
    prompt_count, prompt_rows, model_width = prompt_states.shape
    cycle_index = lax.axis_index("cp")
    cycle_size = lax.axis_size("cp")
    head_count = key_up.shape[1] // HEAD
    lat_half = jnp.dot(
        prompt_states.reshape(prompt_count * prompt_rows, model_width),
        latent_down,
        preferred_element_type=jnp.float32,
    )
    lat_half = lat_half.astype(jnp.bfloat16).reshape(prompt_count, prompt_rows, RANK)
    new_half = jnp.dot(
        decode_states.reshape(STEPS * ROW_GRP, model_width),
        latent_down,
        preferred_element_type=jnp.float32,
    )
    new_half = new_half.astype(jnp.bfloat16).reshape(STEPS, ROW_GRP, RANK)
    latent, new_latent = (
        lax.all_gather(lat_half, "sec", axis=2, tiled=True),
        lax.all_gather(new_half, "sec", axis=2, tiled=True),
    )
    query_pos = row_positions(
        block_order, cycle_index * prompt_rows + jnp.arange(prompt_rows, dtype=jnp.int32)
    )
    queries_abs = absorb(prompt_queries.reshape(prompt_count * prompt_rows, -1), key_up).reshape(
        head_count, prompt_count, prompt_rows, RANK
    )
    start_state = fresh_state((head_count, prompt_count, prompt_rows))
    owners = page_owner[0]
    slot_ids = jnp.arange(PAGES_DEV, dtype=jnp.int32)
    shard_rows = lax.all_gather(latent, "cp", axis=1, tiled=True)
    running = start_state
    running = context_step(running, shard_rows, query_pos, queries_abs, block_order)
    running, whole_store = (running, shard_rows)
    slot_cap = max(1, PAGES_DEV // cycle_size)
    my_owners = lax.dynamic_index_in_dim(owners, cycle_index, 0, keepdims=False)
    same_owner = (my_owners[:, None] == my_owners[None, :]) & (
        slot_ids[None, :] < slot_ids[:, None]
    )
    send_slot = my_owners * slot_cap + jnp.sum(same_owner.astype(jnp.int32), axis=1)
    select = (
        send_slot[None, :] == jnp.arange(cycle_size * slot_cap, dtype=jnp.int32)[:, None]
    ).astype(jnp.bfloat16)
    page_rows = latent.reshape(PAGES_DEV, PAGE * 2 * RANK)
    outgoing = jnp.dot(select, page_rows, preferred_element_type=jnp.float32).astype(jnp.bfloat16)
    outgoing = outgoing.reshape(cycle_size, slot_cap * PAGE, 2 * RANK)
    incoming = lax.all_to_all(outgoing, "cp", split_axis=0, concat_axis=0, tiled=True)
    counts = jnp.sum((owners == cycle_index).astype(jnp.int32), axis=1)
    source_ids = jnp.arange(counts.shape[0], dtype=jnp.int32)
    offsets = jnp.sum(
        jnp.where(source_ids[None, :] < source_ids[:, None], counts[None, :], 0), axis=1
    )
    places = jnp.arange(slot_cap, dtype=jnp.int32)
    slot_valid = places[None, :] < counts[:, None]
    target = jnp.where(slot_valid, offsets[:, None] + places[None, :], -1).reshape(-1)
    compact = (target[None, :] == slot_ids[:, None]).astype(jnp.bfloat16)
    page_store = jnp.dot(
        compact,
        incoming.reshape(cycle_size * slot_cap, PAGE * 2 * RANK),
        preferred_element_type=jnp.float32,
    )
    page_store = page_store.astype(jnp.bfloat16).reshape(PAGES_DEV * PAGE, 2 * RANK)
    final_peak, final_total, final_sum = running
    prefill_latent = (
        (final_sum / final_total[..., None])
        .astype(jnp.bfloat16)
        .reshape(head_count, prompt_count * prompt_rows, RANK)
    )
    prefill_rows = rebuild(prefill_latent, value_up).reshape(
        prompt_count, prompt_rows, head_count * HEAD
    )
    live_rows = query_pos[None, :] < prompt_lengths[:, None]
    prefill_out = jnp.where(live_rows[..., None], prefill_rows, jnp.zeros_like(prefill_rows))
    rows_all = STEPS * ROW_GRP
    score_scale = HEAD ** (-0.5)
    decode_abs = absorb(decode_queries.reshape(rows_all, -1), key_up)
    row_prompt = jnp.arange(ROW_GRP, dtype=jnp.int32) // (ROW_GRP // PPG)
    row_limit = jnp.minimum(decode_context, lookup(prompt_lengths, row_prompt))
    step_abs = decode_abs.reshape(head_count, STEPS, ROW_GRP, RANK)
    own_scores = (
        jnp.einsum(
            "htnr,snr->htns", step_abs, new_latent[..., :RANK], preferred_element_type=jnp.float32
        )
        * score_scale
    )
    step_ids = jnp.arange(STEPS, dtype=jnp.int32)
    own_mask = (step_ids[None, :] <= step_ids[:, None])[:, None, :]
    own_values = new_latent[..., RANK:]

    def weigh_own(weights):
        return jnp.einsum("htns,snr->htnr", weights, own_values, preferred_element_type=jnp.float32)

    own_part = online(fresh_state((head_count, STEPS, ROW_GRP)), own_scores, own_mask, weigh_own)
    own_part = (
        own_part[0].reshape(head_count, rows_all),
        own_part[1].reshape(head_count, rows_all),
        own_part[2].reshape(head_count, rows_all, RANK),
    )
    share_rows = rows_all // cycle_size
    share_start = cycle_index * share_rows
    share_abs = lax.dynamic_slice_in_dim(decode_abs, share_start, share_rows, 1)
    share_ids = (share_start + jnp.arange(share_rows, dtype=jnp.int32)) % ROW_GRP
    share_prompt = lookup(row_prompt, share_ids)
    share_limit = lookup(row_limit, share_ids)
    whole_rows = whole_store.shape[1]
    whole_pos = row_positions(block_order, jnp.arange(whole_rows, dtype=jnp.int32))
    key_prompt = jnp.broadcast_to(
        jnp.arange(prompt_count, dtype=jnp.int32)[:, None], (prompt_count, whole_rows)
    ).reshape(-1)
    key_pos = jnp.broadcast_to(whole_pos[None, :], (prompt_count, whole_rows)).reshape(-1)
    flat_whole = whole_store.reshape(prompt_count * whole_rows, 2 * RANK)
    whole_mask = (key_prompt[None, :] == share_prompt[:, None]) & (
        key_pos[None, :] < share_limit[:, None]
    )
    whole_scores = (
        jnp.einsum(
            "hqr,mr->hqm", share_abs, flat_whole[:, :RANK], preferred_element_type=jnp.float32
        )
        * score_scale
    )
    whole_values = flat_whole[:, RANK:]

    def weigh_whole(weights):
        return jnp.einsum("hqm,mr->hqr", weights, whole_values, preferred_element_type=jnp.float32)

    whole_part = online(
        fresh_state((head_count, share_rows)), whole_scores, whole_mask, weigh_whole
    )
    own_share = tuple(
        (lax.dynamic_slice_in_dim(member, share_start, share_rows, 1) for member in own_part)
    )
    final_peak, final_total, final_sum = combine_parts(whole_part, own_share)
    decoded = rebuild((final_sum / final_total[..., None]).astype(jnp.bfloat16), value_up)
    decoded = lax.all_gather(decoded, "cp", axis=0, tiled=True)
    decode_out = decoded.reshape(STEPS, ROW_GRP, head_count * HEAD)
    page_cache = page_store.reshape(1, 1, PAGES_DEV * PAGE, 2 * RANK)
    return (prefill_out, decode_out, page_cache)


MESH = pl.DeviceIdType.MESH
SCHEDULES = {(4, 2): [('attend', [0], 0), ('receive', 1, 0), ('attend', [0], 1), ('receive', 1, 1), ('own', 0, 0), ('own', 0, 1), ('attend', [1], 0), ('receive', 3, 0), ('attend', [1], 1), ('receive', 3, 1), ('attend', [2], 0), ('pick', 0, 0), ('receive', 2, 0), ('attend', [2], 1), ('receive', 2, 1), ('attend', [3], 0), ('finish', 0, 0), ('attend', [3], 1), ('finish', 0, 1)]}
KEY_LIMIT = 1024


def fused_kernel(
    n,
    k_chunks,
    lengths_hbm,
    order_hbm,
    context_hbm,
    owner_hbm,
    states_hbm,
    fresh_hbm,
    down_hbm,
    queries_hbm,
    asks_hbm,
    key_up_hbm,
    value_up_hbm,
    store_ref,
    prefill_ref,
    decode_ref,
    pick_ref,
    lengths_ref,
    order_ref,
    context_ref,
    owner_ref,
    states_buf,
    fresh_buf,
    down_buf,
    queries_ref,
    asks_ref,
    key_up_ref,
    value_up_ref,
    new_ref,
    absorbed_ref,
    asked_ref,
    peak_ref,
    total_ref,
    sum_ref,
    pick_buf,
    pick_sem,
    load_sem,
    small_sem,
    send_sem,
    recv_sem,
    new_send,
    new_recv,
):
    z = lax.axis_index("cp")
    c = lax.axis_index("sec")
    other = 1 - c
    prompts, rows, width = states_hbm.shape
    heads = key_up_ref.shape[1] // HEAD
    steps, row_grp, _ = asks_ref.shape
    share = row_grp // prompts
    blocks = rows // BLOCK
    asking = heads * rows
    fresh_lanes = heads * steps * share
    lanes = asking + fresh_lanes
    factor = HEAD**-0.5 * math.log2(math.e)
    nt = (((1,), (1,)), ((), ()))
    tn = (((0,), (0,)), ((), ()))
    kw = width // k_chunks
    later_chunks = 4

    small = [
        pltpu.make_async_copy(source, held, small_sem.at[i])
        for i, (source, held) in enumerate(
            [
                (order_hbm, order_ref),
                (lengths_hbm, lengths_ref),
                (context_hbm, context_ref),
                (key_up_hbm, key_up_ref),
                (queries_hbm, queries_ref),
                (asks_hbm, asks_ref),
                (value_up_hbm, value_up_ref),
                (owner_hbm, owner_ref),
            ]
        )
    ]
    pick_copy = pltpu.make_async_copy(pick_buf, pick_ref, pick_sem)
    loads = {}
    for copy in small[:3]:
        copy.start()
    for k in range(k_chunks):
        cols = pl.ds(k * kw, kw)
        loads["w", k] = pltpu.make_async_copy(
            down_hbm.at[cols, :], down_buf.at[cols, :], load_sem.at[0, k]
        )
        loads["w", k].start()
        loads[0, k] = pltpu.make_async_copy(
            states_hbm.at[0, :, cols], states_buf.at[0, :, cols], load_sem.at[1, k]
        )
        loads[0, k].start()
    for p in range(1, prompts):
        for k in range(later_chunks):
            cols = pl.ds(k * (width // later_chunks), width // later_chunks)
            loads[p, k] = pltpu.make_async_copy(
                states_hbm.at[p, :, cols], states_buf.at[p, :, cols], load_sem.at[1 + p, k]
            )
            loads[p, k].start()
    loads["d", 0] = pltpu.make_async_copy(fresh_hbm, fresh_buf, load_sem.at[1 + prompts, 0])
    loads["d", 0].start()
    for copy in small[3:]:
        copy.start()

    barrier = pltpu.get_barrier_semaphore()
    pl.semaphore_signal(barrier, inc=1, device_id={"sec": other}, device_id_type=MESH)
    peers = jnp.int32(1)
    for gap in [g for g in range(1, n) if g != 2]:

        @pl.when(z - gap >= 0)
        def _():
            pl.semaphore_signal(barrier, inc=1, device_id={"cp": z - gap}, device_id_type=MESH)

        @pl.when(z + gap < n)
        def _():
            pl.semaphore_signal(barrier, inc=1, device_id={"cp": z + gap}, device_id_type=MESH)

        peers = peers + (z >= gap).astype(jnp.int32) + (z + gap < n).astype(jnp.int32)

    def shard_rows(shard, p):
        return pl.ds(pl.multiple_of((shard * prompts + p) * rows, rows), rows)

    def transfer(half, shard, p, way, index, target):
        piece = store_ref.at[half, shard_rows(shard, p), :]
        return pltpu.make_async_remote_copy(
            src_ref=piece,
            dst_ref=piece,
            send_sem=send_sem.at[way, index, p],
            recv_sem=recv_sem.at[half, shard, p],
            device_id=target,
            device_id_type=MESH,
        )

    def rightward(shard, p):
        return transfer(c, shard, p, 0, shard, {"cp": z + 1})

    def leftward(shard, p):
        return transfer(c, shard, p, 1, shard, {"cp": z - 1})

    def across(shard, p):
        return transfer(c, shard, p, 2, shard, {"sec": other})

    def direct(target, p):
        return transfer(c, z, p, 3, target, {"cp": target})

    def arrival(shard, p):
        return transfer(c, shard, p, 0, shard, {"cp": z})

    def wait_other(shard, p):
        transfer(other, shard, p, 2, shard, {"sec": other}).wait_recv()

    def project(kind, buf):
        chunks = {0: k_chunks, "d": 1}.get(kind, later_chunks)
        step = width // chunks
        total = jnp.zeros((buf.shape[0], down_buf.shape[1]), jnp.float32)
        for k in range(chunks):
            if kind == 0:
                loads["w", k].wait()
            loads[kind, k].wait()
            cols = pl.ds(k * step, step)
            total += jnp.dot(
                buf[:, cols], down_buf[cols, :], preferred_element_type=jnp.float32
            )
        return total.astype(jnp.bfloat16)

    def stacked(parts):
        return jnp.concatenate(parts, axis=0)

    def head_cols(h):
        return pl.ds(h * HEAD, HEAD)

    def absorb_head(rows_in, h):
        return lax.dot_general(
            key_up_ref[:, head_cols(h)], rows_in, nt, preferred_element_type=jnp.float32
        ).astype(jnp.bfloat16)

    def rebuild_head(rows_in, h):
        return jnp.dot(
            rows_in, value_up_ref[:, head_cols(h)], preferred_element_type=jnp.float32
        ).astype(jnp.bfloat16)

    def place(shard, column):
        row = lax.broadcasted_iota(jnp.int32, (rows, 1) if column else (1, asking), 1 - column)
        row = row if column else row % rows
        found = jnp.zeros_like(row)
        for b in range(blocks):
            shift = (order_ref[shard * blocks + b] - b) * BLOCK
            found = jnp.where(row // BLOCK == b, row + shift, found)
        return found

    for copy in small[:3]:
        copy.wait()
    asked_rows = place(z, 0)
    spot = lax.broadcasted_iota(jnp.int32, (1, fresh_lanes), 1)
    for p in range(prompts):
        asked_ref[p, :, pl.ds(0, asking)] = asked_rows
        limit = jnp.zeros((1, fresh_lanes), jnp.int32)
        for r in range(share):
            limit = jnp.where(
                spot % share == r,
                jnp.minimum(context_ref[p * share + r], lengths_ref[p]) - 1,
                limit,
            )
        asked_ref[p, :, pl.ds(asking, fresh_lanes)] = limit

    for p in range(prompts):
        store_ref[c, shard_rows(z, p), :] = project(p, states_buf.at[p])
        if p == 0:
            pl.semaphore_wait(barrier, peers)

        @pl.when(z > 0)
        def _():
            leftward(z, p).start()

        @pl.when(z < n - 1)
        def _():
            rightward(z, p).start()

        across(z, p).start()
        for gap in range(3, n):

            @pl.when(z - gap >= 0)
            def _():
                direct(z - gap, p).start()

            @pl.when(z + gap < n)
            def _():
                direct(z + gap, p).start()

    new_ref[c] = project("d", fresh_buf)
    new_copy = pltpu.make_async_remote_copy(
        src_ref=new_ref.at[c],
        dst_ref=new_ref.at[c],
        send_sem=new_send,
        recv_sem=new_recv,
        device_id={"sec": other},
        device_id_type=MESH,
    )
    new_copy.start()

    for copy in small[3:]:
        copy.wait()
    for p in range(prompts):
        pieces = [absorb_head(queries_ref[p, :, head_cols(h)], h) for h in range(heads)]
        for h in range(heads):
            asks = [asks_ref[t, pl.ds(p * share, share), head_cols(h)] for t in range(steps)]
            pieces.append(absorb_head(stacked(asks), h))
        absorbed_ref[p] = jnp.concatenate(pieces, axis=1)

    fresh_at = pl.ds(asking, fresh_lanes)
    step_of = spot // share % steps

    def attend_own(p):
        mine = [pl.ds(t * row_grp + p * share, share) for t in range(steps)]
        wide = absorbed_ref[p, :, fresh_at].astype(jnp.float32)
        own_scores = []
        for t in range(steps):
            own_key = stacked([new_ref[0, mine[t], :].astype(jnp.float32)] * (heads * steps)).T
            own = jnp.sum(wide * own_key, axis=0, keepdims=True)
            own_scores.append(jnp.where(step_of >= t, own, NEG))
        old_peak = peak_ref[p, :, fresh_at]
        peak = functools.reduce(jnp.maximum, own_scores, old_peak)
        rescale = jnp.exp2((old_peak - peak) * factor)
        total = total_ref[p, :, fresh_at] * rescale
        summed = sum_ref[p, :, fresh_at] * rescale
        for t in range(steps):
            own_weight = jnp.exp2((own_scores[t] - peak) * factor)
            total = total + own_weight
            own_value = stacked([new_ref[1, mine[t], :].astype(jnp.float32)] * (heads * steps)).T
            summed = summed + own_weight.astype(jnp.bfloat16).astype(jnp.float32) * own_value
        peak_ref[p, :, fresh_at] = peak
        total_ref[p, :, fresh_at] = total
        sum_ref[p, :, fresh_at] = summed

    def attend(shards, p, first=False):
        for shard in shards:
            wait_other(shard, p)
        key_rows = stacked([store_ref[0, shard_rows(shard, p), :] for shard in shards])
        value_rows = stacked([store_ref[1, shard_rows(shard, p), :] for shard in shards])
        scores = jnp.dot(key_rows, absorbed_ref[p], preferred_element_type=jnp.float32)
        asked = asked_ref[p]
        if first:
            key_pos = stacked([place(shard, 1) for shard in shards])
            scores = jnp.where(key_pos <= asked, scores, NEG)
            peak = jnp.max(scores, axis=0, keepdims=True)
            weights = jnp.exp2((scores - peak) * factor)
        else:
            seen = scores[:, :asking]
            starts = [order_ref[shard * blocks + b] * BLOCK for shard in shards for b in range(blocks)]
            allowed = [start <= asked[:, :asking] for start in starts]
            tiles = [seen[b * BLOCK : (b + 1) * BLOCK] for b in range(len(starts))]
            tops = [
                jnp.where(allow, jnp.max(tile, axis=0, keepdims=True), NEG)
                for allow, tile in zip(allowed, tiles)
            ]
            key_pos = stacked([place(shard, 1) for shard in shards])
            fresh = jnp.where(key_pos <= asked[:, asking:], scores[:, asking:], NEG)
            top = jnp.concatenate(
                [functools.reduce(jnp.maximum, tops), jnp.max(fresh, axis=0, keepdims=True)], axis=1
            )
            old_peak = peak_ref[p]
            peak = jnp.maximum(old_peak, top)
            rescale = jnp.exp2((old_peak - peak) * factor)
            weights = jnp.concatenate(
                [
                    stacked(
                        [
                            jnp.exp2((tile - jnp.where(allow, peak[:, :asking], -NEG)) * factor)
                            for allow, tile in zip(allowed, tiles)
                        ]
                    ),
                    jnp.exp2((fresh - peak[:, asking:]) * factor),
                ],
                axis=1,
            )
        total = jnp.sum(weights, axis=0, keepdims=True)
        summed = lax.dot_general(
            value_rows, weights.astype(jnp.bfloat16), tn, preferred_element_type=jnp.float32
        )
        if not first:
            total = total_ref[p] * rescale + total
            summed = sum_ref[p] * rescale + summed
        peak_ref[p] = peak
        total_ref[p] = total
        sum_ref[p] = summed

    def finish(p):
        latent_out = (sum_ref[p] * (1.0 / total_ref[p])).T.astype(jnp.bfloat16)
        live = place(z, 1) < lengths_ref[p]
        for h in range(heads):
            rebuilt = rebuild_head(latent_out[h * rows : (h + 1) * rows], h)
            prefill_ref[p, :, head_cols(h)] = jnp.where(live, rebuilt, jnp.zeros_like(rebuilt))
            first = asking + h * steps * share
            rebuilt = rebuild_head(latent_out[first : first + steps * share], h)
            for t in range(steps):
                decode_ref[t, pl.ds(p * share, share), head_cols(h)] = rebuilt[
                    t * share : (t + 1) * share
                ]

    def pick_slots():
        slot = lax.broadcasted_iota(jnp.int32, (1, pick_buf.shape[1]), 1)
        picked = jnp.zeros_like(slot)
        count = jnp.int32(0)
        for s in range(n):
            for k in range(owner_ref.shape[2]):
                mine = owner_ref[0, s, k] == z
                picked = jnp.where(slot == jnp.where(mine, count, -1), s * owner_ref.shape[2] + k, picked)
                count = count + mine.astype(jnp.int32)
        pick_buf[...] = picked
        pick_copy.start()

    def receive(gap, p):
        @pl.when(z - gap >= 0)
        def _():
            arrival(z - gap, p).wait_recv()
            if gap == 1:

                @pl.when(z < n - 1)
                def _():
                    rightward(z - gap, p).start()

            across(z - gap, p).start()

        @pl.when(z + gap < n)
        def _():
            arrival(z + gap, p).wait_recv()
            if gap == 1:

                @pl.when(z > 0)
                def _():
                    leftward(z + gap, p).start()

            across(z + gap, p).start()

    gaps = [g for g in range(1, n) if g != 2] + [g for g in range(2, min(n, 3))]

    def source(step):
        found, passed = jnp.int32(0), jnp.int32(0)
        for gap in gaps:
            for shard, there in ((z - gap, z >= gap), (z + gap, z + gap < n)):
                passed = passed + there.astype(jnp.int32)
                found = jnp.where(there & (passed == step), shard, found)
        return found

    plan = SCHEDULES.get((n, prompts)) or (
        [("receive", gap, p) for gap in range(1, n) for p in range(prompts)]
        + [("attend", [step], p) for step in range(n) for p in range(prompts)]
        + [("own", 0, p) for p in range(prompts)]
        + [("pick", 0, 0)]
        + [("finish", 0, p) for p in range(prompts)]
    )
    begun = set()
    waited = False
    for kind, which, p in plan:
        if kind == "receive":
            receive(which, p)
        elif kind == "attend":
            attend([source(step) if step else z for step in which], p, first=p not in begun)
            begun.add(p)
        elif kind == "own":
            if not waited:
                new_copy.wait_recv()
                waited = True
            attend_own(p)
        elif kind == "finish":
            finish(p)
        else:
            pick_slots()

    for shard in range(n):
        for p in range(prompts):
            across(shard, p).wait_send()

            @pl.when((shard <= z) & (shard >= z - 1) & (z < n - 1))
            def _():
                rightward(shard, p).wait_send()

            @pl.when((shard >= z) & (shard <= z + 1) & (z > 0))
            def _():
                leftward(shard, p).wait_send()

            @pl.when((shard >= z + 3) | (shard <= z - 3))
            def _():
                direct(shard, p).wait_send()

    new_copy.wait_send()
    pick_copy.wait()


def hand_over_kernel(
    pick_ref,
    store_ref,
    prefill_ref,
    decode_ref,
    prefill_out,
    decode_out,
    page_out,
    pages_ref,
    sems,
):
    whole = [
        pltpu.make_async_copy(prefill_ref, prefill_out, sems.at[0]),
        pltpu.make_async_copy(decode_ref, decode_out, sems.at[1]),
        pltpu.make_async_copy(pages_ref, page_out, sems.at[2]),
    ]
    for copy in whole[:2]:
        copy.start()
    for slot in range(pages_ref.shape[2] // PAGE):
        page = pl.ds(pl.multiple_of(pick_ref[0, slot] * PAGE, PAGE), PAGE)
        pages_ref[0, 0, pl.ds(slot * PAGE, PAGE), :RANK] = store_ref[0, page, :]
        pages_ref[0, 0, pl.ds(slot * PAGE, PAGE), RANK:] = store_ref[1, page, :]
    whole[2].start()
    for copy in whole:
        copy.wait()


def local_small(
    n,
    prompt_states,
    prompt_queries,
    decode_states,
    decode_queries,
    latent_down,
    key_up,
    value_up,
    prompt_lengths,
    block_order,
    page_owner,
    decode_context,
):
    steps, row_grp, width = decode_states.shape
    prompts, rows, _ = prompt_states.shape
    fresh_rows = steps * row_grp
    heads = key_up.shape[1] // HEAD
    lanes = heads * (rows + steps * (row_grp // prompts))
    k_chunks = 4
    hbm = pl.BlockSpec(memory_space=pltpu.HBM)
    smem = pl.BlockSpec(memory_space=pltpu.SMEM)
    vmem = pl.BlockSpec(memory_space=pltpu.VMEM)
    operands = [
        pltpu.with_memory_space_constraint(array, pltpu.HBM)
        for array in (
            prompt_lengths,
            block_order,
            decode_context,
            page_owner,
            prompt_states,
            decode_states.reshape(fresh_rows, width),
            latent_down,
            prompt_queries,
            decode_queries,
            key_up,
            value_up,
        )
    ]
    dma = pltpu.SemaphoreType.DMA
    slots = pl.cdiv(page_owner.shape[2], 128) * 128
    store, prefill, decoded, picks = pl.pallas_call(
        functools.partial(fused_kernel, n, k_chunks),
        out_shape=(
            pltpu.VMEM((2, n * prompts * rows, RANK), jnp.bfloat16),
            pltpu.VMEM(prompt_queries.shape, jnp.bfloat16),
            pltpu.VMEM(decode_queries.shape, jnp.bfloat16),
            pltpu.SMEM((1, slots), jnp.int32),
        ),
        in_specs=[hbm] * len(operands),
        out_specs=(vmem,) * 3 + (smem,),
        scratch_shapes=[
            pltpu.SMEM(prompt_lengths.shape, jnp.int32),
            pltpu.SMEM(block_order.shape, jnp.int32),
            pltpu.SMEM(decode_context.shape, jnp.int32),
            pltpu.SMEM(page_owner.shape, jnp.int32),
            pltpu.VMEM((prompts, rows, width), jnp.bfloat16),
            pltpu.VMEM((fresh_rows, width), jnp.bfloat16),
            pltpu.VMEM(latent_down.shape, jnp.bfloat16),
            pltpu.VMEM(prompt_queries.shape, jnp.bfloat16),
            pltpu.VMEM(decode_queries.shape, jnp.bfloat16),
            pltpu.VMEM(key_up.shape, jnp.bfloat16),
            pltpu.VMEM(value_up.shape, jnp.bfloat16),
            pltpu.VMEM((2, fresh_rows, RANK), jnp.bfloat16),
            pltpu.VMEM((prompts, RANK, lanes), jnp.bfloat16),
            pltpu.VMEM((prompts, 1, lanes), jnp.int32),
            pltpu.VMEM((prompts, 1, lanes), jnp.float32),
            pltpu.VMEM((prompts, 1, lanes), jnp.float32),
            pltpu.VMEM((prompts, RANK, lanes), jnp.float32),
            pltpu.VMEM((1, slots), jnp.int32),
            dma,
            dma((2 + prompts, k_chunks)),
            dma((8,)),
            dma((4, n, prompts)),
            dma((2, n, prompts)),
            dma,
            dma,
        ],
        compiler_params=pltpu.CompilerParams(
            collective_id=0, has_side_effects=True, vmem_limit_bytes=40 * 1024 * 1024
        ),
        name="gather_attend",
    )(*operands)
    pages_dev = page_owner.shape[2]
    page_shape = (1, 1, pages_dev * PAGE, 2 * RANK)
    return pl.pallas_call(
        hand_over_kernel,
        out_shape=(
            jax.ShapeDtypeStruct(prompt_queries.shape, jnp.bfloat16),
            jax.ShapeDtypeStruct(decode_queries.shape, jnp.bfloat16),
            jax.ShapeDtypeStruct(page_shape, jnp.bfloat16),
        ),
        in_specs=[smem] + [vmem] * 3,
        out_specs=(hbm,) * 3,
        scratch_shapes=[
            pltpu.VMEM(page_shape, jnp.bfloat16),
            dma((3,)),
        ],
        compiler_params=pltpu.CompilerParams(vmem_limit_bytes=8 * 1024 * 1024),
        name="hand_over",
    )(picks, store, prefill, decoded)


def solution(mesh):
    placed = (
        P("grp", "cp", None),
        P("grp", "cp", "sec"),
        P(None, "grp", None),
        P(None, "grp", "sec"),
        P(None, "sec"),
        P(None, "sec"),
        P(None, "sec"),
        P("grp"),
        P(),
        P("grp", None, None),
        P("grp"),
    )
    n = mesh.shape["cp"]

    def on_device(prompt_states, *others):
        if n * prompt_states.shape[1] <= KEY_LIMIT and mesh.shape["sec"] == 2:
            return local_small(n, prompt_states, *others)
        return local(prompt_states, *others)

    return jax.shard_map(
        on_device,
        mesh=mesh,
        in_specs=placed,
        out_specs=(P("grp", "cp", "sec"), P(None, "grp", "sec"), P("grp", "cp", None, None)),
        check_vma=False,
    )
```
